512 devices in a mesh: head: 16 (over z), ctx: 32 (over x, y, core).
Axes of the slice: x: 4, y: 4, z: 16, core: 2. Of those that a mesh axis runs over, the one named last changes fastest.
Arguments:
- head_inputs: bfloat16 [32768, 8192], P('ctx', 'head'), may hold values from -6 to 6
- gate_z: bfloat16 [32768, 8192], P('ctx', 'head'), may hold values from -6 to 6
- input_b: bfloat16 [32768, 1024], P('ctx'), may hold values from -0.039794922 to 0.039794922
- output_c: bfloat16 [32768, 1024], P('ctx'), may hold values from -6 to 6
- log_decay: float32 [32768, 128], P('ctx', 'head'), may hold values from -1 to 0
- lengths: int32 [16], replicated, may hold values from 1 to 8192, 32768 in all
- skip_coef: float32 [128], P('head'), may hold values from 0.5 to 1.5
- norm_gain: float32 [8192], P('head'), may hold values from 0.5 to 1.5
Outputs:
- normed: bfloat16 [32768, 8192], P('ctx', 'head')
The draws below stay inside these ranges and needn't reach their ends.
Inputs may be any that keep to these rules, and one draw needn't show every extreme that they name: `lengths`: requests lie end to end from token 0 and fill all 32768 tokens; the longest has exactly 8192 tokens.
All inputs are finite; a program needn't handle non-finite values.
Results may differ from the reference program's by a relative error of at most 0.0085.
Values sent between devices are 32-bit elements; how exact they have to be, the bound alone decides.
A program may use at most 64 MiB of HBM per device.

```python
import math
import jax
import jax.numpy as jnp
import numpy as np
from jax import lax

HEAD_COUNT = 128
P_SIZE = 64
N = 128
G = 8
TOK_DEV = 1024
BLOCK = 512
REQS = 16
PACKED_TOKENS = 32768
MOST = 8192


def draw_log_decay(key, part):
    random_subkeys = jax.random.split(jax.random.fold_in(key, 7), 7)
    fast_share = 0.5
    selector = jax.random.uniform(random_subkeys[0], (HEAD_COUNT,))
    fast_rate = jnp.exp(jax.random.uniform(random_subkeys[1], (HEAD_COUNT,), minval=jnp.log(1.0 / 50.0), maxval=jnp.log(1.0 / 30.0)))
    slow_rate = jnp.exp(jax.random.uniform(random_subkeys[2], (HEAD_COUNT,), minval=jnp.log(0.05 / MOST), maxval=jnp.log(0.3 / MOST)))
    head_decay_rate = jnp.where(selector < fast_share, fast_rate, slow_rate)
    jaggedness = jax.random.uniform(random_subkeys[3], (PACKED_TOKENS, HEAD_COUNT), minval=0.5, maxval=1.5)
    device_ranges = jnp.exp(jax.random.uniform(random_subkeys[4], (PACKED_TOKENS // TOK_DEV, 1, HEAD_COUNT), minval=-0.7, maxval=0.7))
    device_ranges = jnp.broadcast_to(device_ranges, (PACKED_TOKENS // TOK_DEV, TOK_DEV, HEAD_COUNT)).reshape(PACKED_TOKENS, HEAD_COUNT)
    spike_locations = jax.random.randint(random_subkeys[5], (4,), 0, PACKED_TOKENS)
    spike_strike = jnp.any(jnp.arange(PACKED_TOKENS)[:, None] == spike_locations[None, :], axis=1)
    spike_depth = jax.random.uniform(random_subkeys[6], (PACKED_TOKENS, HEAD_COUNT), minval=0.22, maxval=0.69)
    spike_falloff = jnp.where(spike_strike[:, None], spike_depth, 0.0)
    sampled_values = -(head_decay_rate[None, :] * jaggedness * device_ranges) - spike_falloff
    return sampled_values.astype(jnp.float32)


def levels(key, dims, cuts, smallest, high):
    level, own = 1.0, jax.random.fold_in(key, 6)
    for dim, parts in cuts:
        heights = jnp.exp(jax.random.uniform(jax.random.fold_in(own, dim), (parts,), jnp.float32, smallest / len(cuts), high / len(cuts)))
        level = level * jnp.repeat(heights, dims[dim] // parts).reshape([-1 if axis == dim else 1 for axis in range(len(dims))])
    return level


def split_up(amount, total, limit, skew):
    loads = [(1 << 20) // math.isqrt(rank ** skew) + 1 for rank in range(2, amount + 1)]
    surplus, counts = total - limit - (amount - 1), [1] * (amount - 1)
    while surplus > 0:
        movable = [i for i in range(amount - 1) if counts[i] < limit]
        pool, budget = sum([loads[i] for i in movable]), surplus
        for i in movable:
            extra = min(limit - counts[i], max(1, budget * loads[i] // pool), surplus)
            counts[i] = counts[i] + extra
            surplus = surplus - extra
    return np.array([limit] + counts)


def ragged_sizes(key, number_of, total, reach, slope):
    if number_of == 2:
        one = jax.random.randint(key, (), max(1, total - reach), min(reach, total - 1) + 1)
        return jnp.stack([one, total - one])
    sizes = jnp.asarray(split_up(number_of, total, reach, slope), jnp.int32)
    pairs = (number_of - 1) // 2
    source_of, receiver = sizes[1:1 + 2 * pairs:2], sizes[2:2 + 2 * pairs:2]
    slack = jnp.minimum(source_of - 1, reach - receiver)
    moved = jax.random.randint(jax.random.fold_in(key, 1), (pairs,), 0, 1 << 20) % (slack + 1)
    sizes = sizes.at[1:1 + 2 * pairs:2].set(source_of - moved).at[2:2 + 2 * pairs:2].set(receiver + moved)
    return sizes[jax.random.permutation(jax.random.fold_in(key, 2), number_of)]


def normal_values(stream_key, shape, deviation, bound, pieces=(), kind=jnp.bfloat16):
    drawn = jax.random.normal(stream_key, shape, jnp.float32) * deviation
    if len(pieces) > 0:
        drawn = levels(stream_key, shape, pieces, -0.22, 0.18) * drawn
    return jnp.clip(drawn, min=-bound, max=bound).astype(kind)


def setup_inputs(seed: int = 0) -> dict:
    streams_of = jax.random.split(jax.random.key(seed), 9)
    return {
        "head_inputs": normal_values(streams_of[0], (PACKED_TOKENS, HEAD_COUNT * P_SIZE), 1.0, 6.0, ((0, 32), (1, 16))),
        "gate_z": normal_values(streams_of[1], (PACKED_TOKENS, HEAD_COUNT * P_SIZE), 1.0, 6.0, ((0, 32), (1, 16))),
        "input_b": normal_values(streams_of[2], (PACKED_TOKENS, G * N), 0.0062, 0.039794922, ((0, 32),)),
        "output_c": normal_values(streams_of[3], (PACKED_TOKENS, G * N), 1.0, 6.0, ((0, 32),)),
        "log_decay": draw_log_decay(jax.random.fold_in(streams_of[8], 71), 0),
        "lengths": ragged_sizes(streams_of[5], REQS, PACKED_TOKENS, MOST, 2).astype(jnp.int32),
        "skip_coef": jnp.clip(0.5 + 1.0 * jax.random.uniform(streams_of[6], (HEAD_COUNT,), jnp.float32) ** levels(streams_of[6], (HEAD_COUNT,), ((0, 16),), -0.2, 0.2), 0.5, 1.5),
        "norm_gain": jnp.clip(1.0 + 0.1 * jax.random.normal(streams_of[7], (HEAD_COUNT * P_SIZE,), jnp.float32), 0.5, 1.5),
    }


def block_terms(inputs_block, bmaps_block, cmaps_block, decay_block, request_block, prior_request):
    per_group = HEAD_COUNT // G
    group_of = jnp.arange(HEAD_COUNT) // per_group
    cum_decay = jnp.cumsum(decay_block, axis=0).T
    visible = (request_block[:, None] == request_block[None, :]) & (jnp.arange(BLOCK)[:, None] >= jnp.arange(BLOCK)[None, :])
    gaps = cum_decay[:, :, None] - cum_decay[:, None, :]
    decay_matrix = jnp.exp(jnp.where(visible[None], gaps, -jnp.inf))
    scores = jnp.einsum('tgn,sgn->gts', cmaps_block.astype(jnp.float32), bmaps_block.astype(jnp.float32))
    weights = (decay_matrix * scores[group_of]).astype(jnp.bfloat16)
    wide_inputs = inputs_block.astype(jnp.float32)
    inner_part = jnp.einsum('hts,shp->thp', weights.astype(jnp.float32), wide_inputs)
    live_end = request_block == request_block[-1]
    end_weight = jnp.where(live_end[None, :], jnp.exp(cum_decay[:, -1:] - cum_decay), 0.0)
    scaled = (end_weight.T[:, :, None] * bmaps_block.astype(jnp.float32)[:, group_of, :]).astype(jnp.bfloat16)
    block_state = jnp.einsum('shn,shp->hpn', scaled.astype(jnp.float32), wide_inputs)
    block_decay = jnp.where(request_block[-1] == prior_request, jnp.exp(cum_decay[:, -1]), 0.0)
    carry_coef = jnp.where((request_block == prior_request)[:, None], jnp.exp(cum_decay.T), 0.0)
    return (inner_part, block_state, block_decay, carry_coef)

def reference(head_inputs, gate_z, input_b, output_c, log_decay, lengths, skip_coef, norm_gain):
    per_group = HEAD_COUNT // G
    group_of = jnp.arange(HEAD_COUNT) // per_group
    starts = (jnp.cumsum(lengths) - lengths).astype(jnp.int32)
    positions = jnp.arange(PACKED_TOKENS, dtype=jnp.int32)
    request_of = (lax.optimization_barrier(jnp.sum((starts[None, :] <= positions[:, None]).astype(jnp.int32), axis=1)) - 1).astype(jnp.int32)
    block_count = PACKED_TOKENS // BLOCK
    prior_requests = jnp.concatenate([jnp.full((1,), -1, jnp.int32), request_of.reshape(block_count, BLOCK)[:-1, -1]])
    inputs_blocks = head_inputs.reshape(block_count, BLOCK, HEAD_COUNT, P_SIZE)
    bmaps_blocks = input_b.reshape(block_count, BLOCK, G, N)
    cmaps_blocks = output_c.reshape(block_count, BLOCK, G, N)
    decay_blocks = log_decay.reshape(block_count, BLOCK, HEAD_COUNT)
    request_blocks = request_of.reshape(block_count, BLOCK)

    def block_step(running, element):
        inputs_block, bmaps_block, cmaps_block, decay_block, request_block, prior_request = element
        inner_part, block_state, block_decay, carry_coef = block_terms(inputs_block, bmaps_block, cmaps_block, decay_block, request_block, prior_request)
        carried = jnp.einsum('thn,hpn->thp', cmaps_block.astype(jnp.float32)[:, group_of, :], running, precision=lax.Precision.HIGHEST)
        ssd_output = inner_part + skip_coef[None, :, None] * inputs_block.astype(jnp.float32) + carry_coef[:, :, None] * carried
        next_state = block_decay[:, None, None] * running + block_state
        return (next_state, ssd_output.astype(jnp.bfloat16))
    zero_state = jnp.zeros((HEAD_COUNT, P_SIZE, N), jnp.float32)
    final_state, ssd_output = lax.scan(block_step, zero_state, (inputs_blocks, bmaps_blocks, cmaps_blocks, decay_blocks, request_blocks, prior_requests))
    ssd_output = ssd_output.reshape(PACKED_TOKENS, HEAD_COUNT * P_SIZE)
    gated_output = ssd_output.astype(jnp.float32) * jax.nn.silu(gate_z.astype(jnp.float32))
    mean_square = lax.optimization_barrier(jnp.mean(gated_output * gated_output, axis=1, keepdims=True))
    normed = gated_output * lax.rsqrt(mean_square + 1e-05)
    return (normed * norm_gain[None, :]).astype(jnp.bfloat16)
```

```python
import functools

import jax
import jax.numpy as jnp
from jax import lax
from jax.experimental import pallas as pl
from jax.experimental.pallas import tpu as pltpu
from jax.sharding import PartitionSpec as P

MESH = pl.DeviceIdType.MESH
CHUNK = 128
HALF = CHUNK // 2
ROWS = 8
EPS = 1e-05
TO_END, TO_KEY, TO_QUERY, FROM_CHUNK, FROM_DEVICE = range(5)
KINDS = 5
REQUEST_ROW = KINDS * ROWS
F32, BF16 = jnp.float32, jnp.bfloat16


def iota(shape, dim):
    return lax.broadcasted_iota(jnp.int32, shape, dim)


def matmul(left, right):
    return jnp.dot(left, right, preferred_element_type=F32)


def kernel(
    nh, nc, group_heads, lengths, skip, x_hbm, z_hbm, b_hbm, c_hbm, decay_hbm, gain_hbm, out_hbm,
    x, z, b, c, decay, gain, out, table, spread, spread_request, requests, local_state, state,
    partial, gate, decay_out, decay_in, slice_out, slice_in, enter_out, enter_in, square_out, square_in,
    load_sem, store_sem, send_sem, recv_sem,
):
    head_pos = lax.axis_index("head")
    ctx_pos = lax.axis_index("ctx")
    tokens, lanes = x.shape
    chunks = tokens // CHUNK
    width = lanes // ROWS
    state_size = b.shape[1]
    share = slice_in.shape[2]
    share_rows = slice_in.shape[1]
    group = head_pos * ROWS // group_heads
    columns = pl.ds(pl.multiple_of(group * state_size, state_size), state_size)
    loads = [
        pltpu.make_async_copy(decay_hbm, decay, load_sem.at[0]),
        pltpu.make_async_copy(x_hbm, x, load_sem.at[1]),
        pltpu.make_async_copy(b_hbm.at[:, columns], b, load_sem.at[2]),
        pltpu.make_async_copy(c_hbm.at[:, columns], c, load_sem.at[3]),
        pltpu.make_async_copy(z_hbm, z, load_sem.at[4]),
        pltpu.make_async_copy(gain_hbm, gain, load_sem.at[5]),
    ]
    for load in loads:
        load.start()

    barrier = pltpu.get_barrier_semaphore()

    def greet(axis, place, count):
        def one(step, carry):
            pl.semaphore_signal(
                barrier, inc=1, device_id={axis: lax.rem(place + step, count)}, device_id_type=MESH
            )
            return carry

        lax.fori_loop(1, count, one, 0)

    greet("ctx", ctx_pos, nc)
    greet("head", head_pos, nh)

    def exchange(axis, place, count, source, target, which):
        def one(step, carry):
            other = lax.rem(place + step, count)
            pltpu.make_async_remote_copy(
                src_ref=source(other),
                dst_ref=target.at[place],
                send_sem=send_sem.at[which],
                recv_sem=recv_sem.at[which],
                device_id={axis: other},
                device_id_type=MESH,
            ).start()
            return carry

        lax.fori_loop(1, count, one, 0)

    def arrival(axis, place, count, target, which):
        return pltpu.make_async_remote_copy(
            src_ref=target.at[pl.ds(0, count - 1)],
            dst_ref=target.at[pl.ds(0, count - 1)],
            send_sem=send_sem.at[which],
            recv_sem=recv_sem.at[which],
            device_id={axis: lax.rem(place + 1, count)},
            device_id_type=MESH,
        )

    starts = []
    running = jnp.int32(0)
    for r in range(lengths.shape[0]):
        starts.append(running)
        running = running + lengths[r]

    def request_at(position):
        total = jnp.zeros(position.shape, F32)
        for start in starts:
            total = total + jnp.where(position >= start, 1.0, 0.0)
        return total

    chunk_first = ctx_pos * tokens + iota((chunks, CHUNK), 0) * CHUNK
    request = request_at(chunk_first + iota((chunks, CHUNK), 1))
    request_end = request_at(chunk_first + (CHUNK - 1))
    request_prior = request_at(chunk_first - 1)
    live_end = jnp.where(request == request_end, 1.0, 0.0)
    live_start = jnp.where(request == request_prior, 1.0, 0.0)
    requests[...] = request

    row = iota((CHUNK, lanes), 0)
    row = jnp.where(row >= HALF, row - HALF, row)
    head_of_lane = iota((CHUNK, lanes), 1) // width
    for kind in range(KINDS):
        spread[kind] = jnp.where(row == kind * ROWS + head_of_lane, 1.0, 0.0).astype(BF16)
    spread_request[...] = jnp.where(iota((CHUNK, CHUNK), 0) == REQUEST_ROW, 1.0, 0.0).astype(BF16)
    lane_head = iota((1, lanes), 1) // width
    skip_row = jnp.zeros((1, lanes), F32)
    for h in range(ROWS):
        skip_row = jnp.where(lane_head == h, skip[h], skip_row)

    loads[0].wait()
    upper = jnp.where(iota((CHUNK, CHUNK), 0) <= iota((CHUNK, CHUNK), 1), 1.0, 0.0)
    stacked = jnp.concatenate([decay[:, k * CHUNK : (k + 1) * CHUNK] for k in range(chunks)], axis=0)
    cum = jnp.dot(stacked, upper, preferred_element_type=F32, precision=lax.Precision.HIGHEST)
    before = jnp.ones((ROWS, CHUNK), F32)
    for k in range(chunks):
        part = cum[k * ROWS : (k + 1) * ROWS]
        middle = jnp.broadcast_to(part[:, HALF - 1 : HALF], part.shape)
        end = jnp.broadcast_to(part[:, CHUNK - 1 :], part.shape)
        from_start = jnp.exp(part) * live_start[k : k + 1]
        factors = [
            jnp.exp(end - part) * live_end[k : k + 1],
            jnp.exp(middle - part),
            jnp.exp(part - middle),
            from_start,
            from_start * before,
        ]
        before = before * jnp.broadcast_to(from_start[:, CHUNK - 1 :], part.shape)
        values = jnp.concatenate(factors, axis=0)
        high = values.astype(BF16).astype(F32)
        request_rows = jnp.broadcast_to(request[k : k + 1], (ROWS, CHUNK))
        blank = jnp.zeros((HALF - REQUEST_ROW - ROWS, CHUNK), F32)
        blank_low = jnp.zeros((HALF - REQUEST_ROW, CHUNK), F32)
        whole = jnp.concatenate([high, request_rows, blank, values - high, blank_low], axis=0)
        table[k] = whole.T.astype(BF16)

    def last_row(k, kind):
        return matmul(table[k, CHUNK - 16 :, :], spread[kind])[15:16]

    decay_out[...] = last_row(chunks - 1, FROM_DEVICE)

    loads[1].wait()
    loads[2].wait()
    state[...] = jnp.zeros(state.shape, F32)

    def at(k):
        return pl.ds(pl.multiple_of(k * CHUNK, CHUNK), CHUNK)

    def add_state(k, carry):
        local_state[k] = state[...].astype(BF16)
        scaled = (x[at(k), :].astype(F32) * matmul(table[k], spread[TO_END])).astype(BF16)
        added = lax.dot_general(
            b[at(k), :], scaled, (((0,), (0,)), ((), ())), preferred_element_type=F32
        )
        state[...] = last_row(k, FROM_CHUNK) * state[...] + added
        return carry

    lax.fori_loop(0, chunks, add_state, 0)
    halves = lanes // share
    for i in range(nc):
        top, left = (i // halves) * share_rows, (i % halves) * share
        slice_out[i] = state[top : top + share_rows, left : left + share]

    pl.semaphore_wait(barrier, nc - 1 + nh - 1)
    exchange("ctx", ctx_pos, nc, lambda other: decay_out, decay_in, 0)
    exchange("ctx", ctx_pos, nc, lambda other: slice_out.at[other], slice_in, 1)
    decay_in[ctx_pos] = decay_out[...]
    slice_in[ctx_pos] = slice_out[ctx_pos]

    loads[3].wait()
    loads[4].wait()
    causal = iota((CHUNK, CHUNK), 0) >= iota((CHUNK, CHUNK), 1)

    def own_part(k, carry):
        rows = at(k)
        maps = c[rows, :]
        scores = lax.dot_general(
            maps, b[rows, :], (((1,), (1,)), ((), ())), preferred_element_type=F32
        )
        same = matmul(table[k], spread_request[...]) == requests[pl.ds(k, 1), :]
        scores = jnp.where(causal & same, scores, 0.0).astype(BF16)
        wide = x[rows, :].astype(F32)
        keys = (wide * matmul(table[k], spread[TO_KEY])).astype(BF16)
        total = matmul(scores, keys) * matmul(table[k], spread[TO_QUERY])
        total += matmul(maps, local_state[k]) * matmul(table[k], spread[FROM_CHUNK])
        partial[rows, :] = total + skip_row * wide
        branch = z[rows, :].astype(F32)
        gate[rows, :] = branch / (1.0 + jnp.exp(-branch))
        return carry

    lax.fori_loop(0, chunks, own_part, 0)

    for target, which in ((decay_in, 0), (slice_in, 1)):
        arrived = arrival("ctx", ctx_pos, nc, target, which)
        arrived.wait_recv()
        arrived.wait_send()
    side = pl.ds(pl.multiple_of(lax.rem(ctx_pos, halves) * share, share), share)

    def scan(i, entering):
        enter_out[i] = entering
        return decay_in[i, :, side] * entering + slice_in[i]

    lax.fori_loop(0, nc, scan, jnp.zeros((share_rows, share), F32))
    exchange("ctx", ctx_pos, nc, lambda other: enter_out.at[other], enter_in, 2)
    enter_in[ctx_pos] = enter_out[ctx_pos]
    arrived = arrival("ctx", ctx_pos, nc, enter_in, 2)
    arrived.wait_recv()
    for i in range(nc):
        top, left = (i // halves) * share_rows, (i % halves) * share
        state[top : top + share_rows, left : left + share] = enter_in[i]
    local_state[0] = state[...].astype(BF16)

    def add_carried(k, carry):
        rows = at(k)
        carried = matmul(c[rows, :], local_state[0]) * matmul(table[k], spread[FROM_DEVICE])
        output = (partial[rows, :] + carried).astype(BF16).astype(F32)
        gated = output * gate[rows, :]
        partial[rows, :] = gated
        squared = gated * gated
        folded = squared[:, :CHUNK]
        for i in range(1, lanes // CHUNK):
            folded = folded + squared[:, i * CHUNK : (i + 1) * CHUNK]
        square_out[pl.ds(k, 1), :] = jnp.sum(folded.T, axis=0, keepdims=True)
        return carry

    lax.fori_loop(0, chunks, add_carried, 0)
    arrived.wait_send()

    exchange("head", head_pos, nh, lambda other: square_out, square_in, 3)
    square_in[head_pos] = square_out[...]
    loads[5].wait()
    arrived = arrival("head", head_pos, nh, square_in, 3)
    arrived.wait_recv()
    squares = square_in[0]
    for i in range(1, nh):
        squares = squares + square_in[i]
    requests[...] = lax.rsqrt(squares / (nh * lanes) + EPS)

    def normalize(k, carry):
        rows = at(k)
        scale = jnp.broadcast_to(requests[pl.ds(k, 1), :], (CHUNK, CHUNK)).T
        scale = jnp.concatenate([scale] * (lanes // CHUNK), axis=1)
        out[rows, :] = (partial[rows, :] * scale * gain[...]).astype(BF16)
        pltpu.make_async_copy(out.at[rows, :], out_hbm.at[rows, :], store_sem).start()
        return carry

    lax.fori_loop(0, chunks, normalize, 0)
    arrived.wait_send()
    pltpu.make_async_copy(out, out_hbm, store_sem).wait()


def on_device(nh, nc, head_inputs, gate_z, input_b, output_c, log_decay, lengths, skip_coef, norm_gain):
    tokens, lanes = head_inputs.shape
    heads = skip_coef.shape[0]
    assert heads == ROWS and tokens == ROWS * CHUNK
    state_size = CHUNK
    groups = input_b.shape[1] // state_size
    chunks = tokens // CHUNK
    share = lanes // 2
    share_rows = 2 * state_size // nc
    vmem, smem, anywhere = pltpu.VMEM, pltpu.SMEM, pl.ANY
    return pl.pallas_call(
        functools.partial(kernel, nh, nc, heads * nh // groups),
        out_shape=jax.ShapeDtypeStruct((tokens, lanes), BF16),
        in_specs=[pl.BlockSpec(memory_space=smem)] * 2 + [pl.BlockSpec(memory_space=anywhere)] * 6,
        out_specs=pl.BlockSpec(memory_space=anywhere),
        scratch_shapes=[
            vmem((tokens, lanes), BF16),
            vmem((tokens, lanes), BF16),
            vmem((tokens, state_size), BF16),
            vmem((tokens, state_size), BF16),
            vmem((heads, tokens), F32),
            vmem((1, lanes), F32),
            vmem((tokens, lanes), BF16),
            vmem((chunks, CHUNK, CHUNK), BF16),
            vmem((KINDS, CHUNK, lanes), BF16),
            vmem((CHUNK, CHUNK), BF16),
            vmem((chunks, CHUNK), F32),
            vmem((chunks, state_size, lanes), BF16),
            vmem((state_size, lanes), F32),
            vmem((tokens, lanes), F32),
            vmem((tokens, lanes), F32),
            vmem((1, lanes), F32),
            vmem((nc, 1, lanes), F32),
            vmem((nc, share_rows, share), F32),
            vmem((nc, share_rows, share), F32),
            vmem((nc, share_rows, share), F32),
            vmem((nc, share_rows, share), F32),
            vmem((chunks, CHUNK), F32),
            vmem((nh, chunks, CHUNK), F32),
            pltpu.SemaphoreType.DMA((6,)),
            pltpu.SemaphoreType.DMA,
            pltpu.SemaphoreType.DMA((4,)),
            pltpu.SemaphoreType.DMA((4,)),
        ],
        compiler_params=pltpu.CompilerParams(collective_id=0, has_side_effects=True),
    )(
        lengths, skip_coef, head_inputs, gate_z, input_b, output_c, log_decay.T,
        norm_gain.reshape(1, lanes),
    )


def solution(mesh):
    return jax.shard_map(
        functools.partial(on_device, mesh.shape["head"], mesh.shape["ctx"]),
        mesh=mesh,
        in_specs=(
            P("ctx", "head"),
            P("ctx", "head"),
            P("ctx", None),
            P("ctx", None),
            P("ctx", "head"),
            P(),
            P("head"),
            P("head"),
        ),
        out_specs=P("ctx", "head"),
        check_vma=False,
    )
```

```python
import functools
import math

import jax
import jax.numpy as jnp
from jax import lax
from jax.experimental import pallas as pl
from jax.experimental.pallas import tpu as pltpu
from jax.sharding import PartitionSpec as P

MESH = pl.DeviceIdType.MESH
CHUNK = 128
HALF = CHUNK // 2
ROWS = 8
EPS = 1e-05
TO_END, TO_KEY, TO_QUERY, FROM_CHUNK, FROM_DEVICE = range(5)
KINDS = 5
REQUEST_ROW = KINDS * ROWS
F32, BF16 = jnp.float32, jnp.bfloat16


def iota(shape, dim):
    return lax.broadcasted_iota(jnp.int32, shape, dim)


def matmul(left, right):
    return jnp.dot(left, right, preferred_element_type=F32)


def around(offset, count):
    return min(offset, count - offset)


def kernel(
    nh, nc, group_heads, lengths_hbm, skip_hbm, x_hbm, z_hbm, b_hbm, c_hbm, decay_hbm, gated, scales,
    lengths, skip, x, z, b, c, b_turned, decay, table, spread, spread_request, requests, leaving, local_state, state,
    partial, gate, from_device, decay_out, decay_in, slice_out, slice_in, enter_out, enter_in,
    square_out, square_in, load_sem, send_sem, recv_sem,
):
    head_pos = lax.axis_index("head")
    ctx_pos = lax.axis_index("ctx")
    tokens, lanes = x.shape
    chunks = tokens // CHUNK
    width = lanes // ROWS
    state_size = b.shape[1]
    share_rows, share = slice_in.shape[1:]
    group = head_pos * ROWS // group_heads
    columns = pl.ds(pl.multiple_of(group * state_size, state_size), state_size)
    loads = [
        pltpu.make_async_copy(decay_hbm, decay, load_sem.at[0]),
        pltpu.make_async_copy(b_hbm.at[:, columns], b, load_sem.at[1]),
        pltpu.make_async_copy(x_hbm, x, load_sem.at[2]),
        pltpu.make_async_copy(c_hbm.at[:, columns], c, load_sem.at[3]),
        pltpu.make_async_copy(z_hbm, z, load_sem.at[4]),
        pltpu.make_async_copy(skip_hbm, skip, load_sem.at[5]),
        pltpu.make_async_copy(lengths_hbm, lengths, load_sem.at[6]),
    ]
    for i in (6, 0, 1, 2, 3, 4, 5):
        loads[i].start()

    barrier = pltpu.get_barrier_semaphore()

    def greet(axis, place, count):
        def one(step, carry):
            pl.semaphore_signal(
                barrier, inc=1, device_id={axis: lax.rem(place + step, count)}, device_id_type=MESH
            )
            return carry

        lax.fori_loop(1, count, one, 0)

    greet("ctx", ctx_pos, nc)
    greet("head", head_pos, nh)

    def send(axis, place, other, source, target, which):
        pltpu.make_async_remote_copy(
            src_ref=source,
            dst_ref=target.at[place],
            send_sem=send_sem.at[which],
            recv_sem=recv_sem.at[which],
            device_id={axis: other},
            device_id_type=MESH,
        ).start()

    side = math.isqrt(nc // 2)
    core = lax.rem(ctx_pos, 2)
    chip_row, chip_column = ctx_pos // (2 * side), lax.rem(ctx_pos // 2, side)
    hops = sorted(
        ((i, j) for i in range(side) for j in range(side)),
        key=lambda hop: -around(hop[0], side) - around(hop[1], side),
    )

    def send_to_core(which_core, source, target, which):
        for down, along in hops:
            chip = lax.rem(chip_row + down, side) * side + lax.rem(chip_column + along, side)
            other = 2 * chip + which_core
            if (down, along) == (0, 0):

                @pl.when(core != which_core)
                def _():
                    send("ctx", ctx_pos, other, source(other), target, which)

            else:
                send("ctx", ctx_pos, other, source(other), target, which)

    def arrival(axis, place, count, target, which):
        return pltpu.make_async_remote_copy(
            src_ref=target.at[pl.ds(0, count - 1)],
            dst_ref=target.at[pl.ds(0, count - 1)],
            send_sem=send_sem.at[which],
            recv_sem=recv_sem.at[which],
            device_id={axis: lax.rem(place + 1, count)},
            device_id_type=MESH,
        )

    loads[6].wait()
    starts = []
    running = jnp.int32(0)
    for r in range(lengths.shape[0]):
        starts.append(running)
        running = running + lengths[r]

    def request_at(position):
        total = jnp.zeros(position.shape, F32)
        for start in starts:
            total = total + jnp.where(position >= start, 1.0, 0.0)
        return total

    chunk_first = ctx_pos * tokens + iota((chunks, CHUNK), 0) * CHUNK
    request = request_at(chunk_first + iota((chunks, CHUNK), 1))
    request_end = request_at(chunk_first + (CHUNK - 1))
    request_prior = request_at(chunk_first - 1)
    live_end = jnp.where(request == request_end, 1.0, 0.0)
    live_start = jnp.where(request == request_prior, 1.0, 0.0)
    requests[...] = request

    row = iota((CHUNK, lanes), 0)
    row = jnp.where(row >= HALF, row - HALF, row)
    head_of_lane = iota((CHUNK, lanes), 1) // width
    for kind in range(KINDS):
        spread[kind] = jnp.where(row == kind * ROWS + head_of_lane, 1.0, 0.0).astype(BF16)
    spread_request[...] = jnp.where(iota((CHUNK, CHUNK), 0) == REQUEST_ROW, 1.0, 0.0).astype(BF16)

    loads[0].wait()
    upper = jnp.where(iota((CHUNK, CHUNK), 0) <= iota((CHUNK, CHUNK), 1), 1.0, 0.0)
    stacked = jnp.concatenate([decay[:, k * CHUNK : (k + 1) * CHUNK] for k in range(chunks)], axis=0)
    cum = jnp.dot(stacked, upper, preferred_element_type=F32, precision=lax.Precision.HIGHEST)
    before = jnp.ones((ROWS, CHUNK), F32)
    for k in range(chunks):
        part = cum[k * ROWS : (k + 1) * ROWS]
        middle = jnp.broadcast_to(part[:, HALF - 1 : HALF], part.shape)
        end = jnp.broadcast_to(part[:, CHUNK - 1 :], part.shape)
        from_start = jnp.exp(part) * live_start[k : k + 1]
        factors = [
            jnp.exp(end - part) * live_end[k : k + 1],
            jnp.exp(middle - part),
            jnp.exp(part - middle),
            from_start,
            from_start * before,
        ]
        before = before * jnp.broadcast_to(from_start[:, CHUNK - 1 :], part.shape)
        values = jnp.concatenate(factors, axis=0)
        high = values.astype(BF16).astype(F32)
        request_rows = jnp.broadcast_to(request[k : k + 1], (ROWS, CHUNK))
        blank = jnp.zeros((HALF - REQUEST_ROW - ROWS, CHUNK), F32)
        blank_low = jnp.zeros((HALF - REQUEST_ROW, CHUNK), F32)
        whole = jnp.concatenate([high, request_rows, blank, values - high, blank_low], axis=0)
        table[k] = whole.T.astype(BF16)
    decay_out[...] = table[chunks - 1, CHUNK - 16 :, :].astype(F32)[15:16]
    leaving[...] = matmul(table[:, CHUNK - 16 :, :].reshape(16 * chunks, CHUNK), spread[FROM_CHUNK])

    loads[1].wait()
    for k in range(chunks):
        b_turned[k] = b[k * CHUNK : (k + 1) * CHUNK, :].T
    loads[2].wait()
    for half in range(2):
        part = slice(half * share, (half + 1) * share)
        entering = jnp.zeros((state_size, share), F32)
        for k in range(chunks):
            rows = slice(k * CHUNK, (k + 1) * CHUNK)
            local_state[k, :, part] = entering.astype(BF16)
            scaled = (x[rows, part].astype(F32) * matmul(table[k], spread[TO_END, :, part])).astype(BF16)
            entering = leaving[16 * k + 15 : 16 * k + 16, part] * entering + matmul(b_turned[k], scaled)
        for i in range(nc // 2):
            slice_out[2 * i + half] = entering[i * share_rows : (i + 1) * share_rows]
        if half == 0:
            pl.semaphore_wait(barrier, nc - 1 + nh - 1)
            for which_core in range(2):
                send_to_core(which_core, lambda other: decay_out, decay_in, 0)
        send_to_core(half, lambda other: slice_out.at[other], slice_in, 1)
    decay_in[ctx_pos] = decay_out[...]
    slice_in[ctx_pos] = slice_out[ctx_pos]

    def at(k):
        return pl.ds(pl.multiple_of(k * CHUNK, CHUNK), CHUNK)

    loads[3].wait()
    loads[4].wait()
    loads[5].wait()
    lane_head = iota((1, lanes), 1) // width
    skip_row = jnp.zeros((1, lanes), F32)
    for h in range(ROWS):
        skip_row = jnp.where(lane_head == h, skip[h], skip_row)
    causal = iota((CHUNK, CHUNK), 0) >= iota((CHUNK, CHUNK), 1)

    def own_part(k, carry):
        rows = at(k)
        maps = c[rows, :]
        same = matmul(table[k], spread_request[...]) == requests[pl.ds(k, 1), :]
        scores = jnp.where(causal & same, matmul(maps, b_turned[k]), 0.0).astype(BF16)
        wide = x[rows, :].astype(F32)
        keys = (wide * matmul(table[k], spread[TO_KEY])).astype(BF16)
        total = matmul(scores, keys) * matmul(table[k], spread[TO_QUERY])
        total += matmul(maps, local_state[k]) * matmul(table[k], spread[FROM_CHUNK])
        partial[rows, :] = total + skip_row * wide
        from_device[rows, :] = matmul(table[k], spread[FROM_DEVICE])
        branch = z[rows, :].astype(F32)
        gate[rows, :] = branch / (1.0 + jnp.exp(-branch))
        return carry

    lax.fori_loop(0, chunks, own_part, 0)

    for target, which in ((decay_in, 0), (slice_in, 1)):
        arrived = arrival("ctx", ctx_pos, nc, target, which)
        arrived.wait_recv()
        arrived.wait_send()
    rows_in = jnp.concatenate([decay_in[i] for i in range(nc)], axis=0).astype(BF16)
    part = pl.ds(pl.multiple_of(core * share, share), share)
    steps = matmul(rows_in, spread[FROM_DEVICE, :, part])
    entering = jnp.zeros((share_rows, share), F32)
    for i in range(nc):
        enter_out[i] = entering
        entering = steps[i : i + 1] * entering + slice_in[i]
    for which_core in range(2):
        send_to_core(which_core, lambda other: enter_out.at[other], enter_in, 2)
    enter_in[ctx_pos] = enter_out[ctx_pos]
    arrived = arrival("ctx", ctx_pos, nc, enter_in, 2)
    arrived.wait_recv()
    for half in range(2):
        for i in range(nc // 2):
            state[i * share_rows : (i + 1) * share_rows, half * share : (half + 1) * share] = enter_in[2 * i + half]
    entered = state[...].astype(BF16)

    step_rows = 2 * CHUNK
    for k in range(tokens // step_rows):
        rows = slice(k * step_rows, (k + 1) * step_rows)
        output = partial[rows, :] + matmul(c[rows, :], entered) * from_device[rows, :]
        gates = output.astype(BF16).astype(F32) * gate[rows, :]
        gated[rows, :] = gates
        squared = gates * gates
        folded = squared[:, :CHUNK]
        for i in range(1, lanes // CHUNK):
            folded = folded + squared[:, i * CHUNK : (i + 1) * CHUNK]
        for i in range(2):
            square_out[2 * k + i : 2 * k + i + 1, :] = jnp.sum(
                folded[i * CHUNK : (i + 1) * CHUNK].T, axis=0, keepdims=True
            )

    for offset in sorted(range(1, nh), key=lambda offset: -around(offset, nh)):
        send("head", head_pos, lax.rem(head_pos + offset, nh), square_out, square_in, 3)
    square_in[head_pos] = square_out[...]
    arrived.wait_send()
    arrived = arrival("head", head_pos, nh, square_in, 3)
    arrived.wait_recv()
    squares = square_in[0]
    for i in range(1, nh):
        squares = squares + square_in[i]
    scales[...] = lax.rsqrt(squares / (nh * lanes) + EPS)
    arrived.wait_send()


def normalize(gated, scales, gain, out_hbm, out, sem):
    tokens, lanes = gated.shape
    copies = []
    for k in range(tokens // CHUNK):
        rows = slice(k * CHUNK, (k + 1) * CHUNK)
        scale = jnp.broadcast_to(scales[k : k + 1, :], (CHUNK, CHUNK)).T
        scale = jnp.concatenate([scale] * (lanes // CHUNK), axis=1)
        out[rows, :] = (gated[rows, :] * scale * gain[...]).astype(BF16)
        copies.append(pltpu.make_async_copy(out.at[rows, :], out_hbm.at[rows, :], sem.at[k]))
        copies[-1].start()
    for copy in copies:
        copy.wait()


def on_device(nh, nc, head_inputs, gate_z, input_b, output_c, log_decay, lengths, skip_coef, norm_gain):
    tokens, lanes = head_inputs.shape
    heads = skip_coef.shape[0]
    assert heads == ROWS and tokens == ROWS * CHUNK
    state_size = CHUNK
    groups = input_b.shape[1] // state_size
    chunks = tokens // CHUNK
    share = lanes // 2
    share_rows = 2 * state_size // nc
    vmem, smem, hbm = pltpu.VMEM, pltpu.SMEM, pltpu.HBM
    gated, scales = pl.pallas_call(
        functools.partial(kernel, nh, nc, heads * nh // groups),
        out_shape=(
            jax.ShapeDtypeStruct((tokens, lanes), F32),
            jax.ShapeDtypeStruct((chunks, CHUNK), F32),
        ),
        in_specs=[pl.BlockSpec(memory_space=hbm)] * 7,
        out_specs=(pl.BlockSpec(memory_space=vmem), pl.BlockSpec(memory_space=vmem)),
        scratch_shapes=[
            smem(lengths.shape, jnp.int32),
            smem(skip_coef.shape, F32),
            vmem((tokens, lanes), BF16),
            vmem((tokens, lanes), BF16),
            vmem((tokens, state_size), BF16),
            vmem((tokens, state_size), BF16),
            vmem((chunks, state_size, CHUNK), BF16),
            vmem((heads, tokens), F32),
            vmem((chunks, CHUNK, CHUNK), BF16),
            vmem((KINDS, CHUNK, lanes), BF16),
            vmem((CHUNK, CHUNK), BF16),
            vmem((chunks, CHUNK), F32),
            vmem((16 * chunks, lanes), F32),
            vmem((chunks, state_size, lanes), BF16),
            vmem((state_size, lanes), F32),
            vmem((tokens, lanes), F32),
            vmem((tokens, lanes), F32),
            vmem((tokens, lanes), F32),
            vmem((1, CHUNK), F32),
            vmem((nc, 1, CHUNK), F32),
            vmem((nc, share_rows, share), F32),
            vmem((nc, share_rows, share), F32),
            vmem((nc, share_rows, share), F32),
            vmem((nc, share_rows, share), F32),
            vmem((chunks, CHUNK), F32),
            vmem((nh, chunks, CHUNK), F32),
            pltpu.SemaphoreType.DMA((7,)),
            pltpu.SemaphoreType.DMA((4,)),
            pltpu.SemaphoreType.DMA((4,)),
        ],
        compiler_params=pltpu.CompilerParams(
            collective_id=0, has_side_effects=True, vmem_limit_bytes=24 << 20
        ),
    )(*(
        pltpu.with_memory_space_constraint(operand, hbm)
        for operand in (lengths, skip_coef, head_inputs, gate_z, input_b, output_c, log_decay.T)
    ))
    return pl.pallas_call(
        normalize,
        out_shape=jax.ShapeDtypeStruct((tokens, lanes), BF16),
        in_specs=[pl.BlockSpec(memory_space=vmem)] * 3,
        out_specs=pl.BlockSpec(memory_space=hbm),
        scratch_shapes=[vmem((tokens, lanes), BF16), pltpu.SemaphoreType.DMA((chunks,))],
        compiler_params=pltpu.CompilerParams(vmem_limit_bytes=8 << 20),
    )(gated, scales, norm_gain.reshape(1, lanes))


def solution(mesh):
    return jax.shard_map(
        functools.partial(on_device, mesh.shape["head"], mesh.shape["ctx"]),
        mesh=mesh,
        in_specs=(
            P("ctx", "head"),
            P("ctx", "head"),
            P("ctx", None),
            P("ctx", None),
            P("ctx", "head"),
            P(),
            P("head"),
            P("head"),
        ),
        out_specs=P("ctx", "head"),
        check_vma=False,
    )
```

```python
import functools
import math

import jax
import jax.numpy as jnp
from jax import lax
from jax.experimental import pallas as pl
from jax.experimental.pallas import tpu as pltpu
from jax.sharding import PartitionSpec as P

MESH = pl.DeviceIdType.MESH
CHUNK = 128
HALF = CHUNK // 2
ROWS = 8
EPS = 1e-05
TO_END, TO_KEY, TO_QUERY, FROM_CHUNK, FROM_DEVICE = range(5)
KINDS = 5
REQUEST_ROW = KINDS * ROWS
F32, BF16 = jnp.float32, jnp.bfloat16


def iota(shape, dim):
    return lax.broadcasted_iota(jnp.int32, shape, dim)


def matmul(left, right):
    return jnp.dot(left, right, preferred_element_type=F32)


def around(offset, count):
    return min(offset, count - offset)


def kernel(
    nh, nc, group_heads, lengths_hbm, skip_hbm, x_hbm, z_hbm, b_hbm, c_hbm, decay_hbm, gated, scales,
    lengths, skip, x, z, b, c, b_turned, decay, table, spread, spread_request, requests, leaving, local_state, state,
    partial, gate, from_device, decay_out, decay_in, slice_out, slice_in, enter_out, enter_in,
    square_out, square_in, load_sem, send_sem, recv_sem, ready,
):
    head_pos = lax.axis_index("head")
    ctx_pos = lax.axis_index("ctx")
    tokens, lanes = x.shape
    chunks = tokens // CHUNK
    width = lanes // ROWS
    state_size = b.shape[1]
    share_rows, share = slice_in.shape[1:]
    group = head_pos * ROWS // group_heads
    columns = pl.ds(pl.multiple_of(group * state_size, state_size), state_size)
    loads = [
        pltpu.make_async_copy(decay_hbm, decay, load_sem.at[0]),
        pltpu.make_async_copy(b_hbm.at[:, columns], b, load_sem.at[1]),
        pltpu.make_async_copy(x_hbm, x, load_sem.at[2]),
        pltpu.make_async_copy(c_hbm.at[:, columns], c, load_sem.at[3]),
        pltpu.make_async_copy(z_hbm, z, load_sem.at[4]),
        pltpu.make_async_copy(skip_hbm, skip, load_sem.at[5]),
        pltpu.make_async_copy(lengths_hbm, lengths, load_sem.at[6]),
    ]
    for i in (6, 0, 1, 2, 3, 4, 5):
        loads[i].start()

    barrier = pltpu.get_barrier_semaphore()

    def greet(step, carry):
        other = lax.rem(ctx_pos + step, nc)
        pl.semaphore_signal(barrier, inc=1, device_id={"ctx": other}, device_id_type=MESH)
        return carry

    def signal_heads(semaphore, distance):
        for offset in (distance, nh - distance):
            pl.semaphore_signal(
                semaphore, inc=1, device_id={"head": lax.rem(head_pos + offset, nh)}, device_id_type=MESH
            )

    lax.fori_loop(1, nc, greet, 0)
    signal_heads(barrier, 1)
    rounds = [2**i for i in range(nh.bit_length()) if 2 * 2**i < nh]

    def send(axis, place, other, source, target, which):
        pltpu.make_async_remote_copy(
            src_ref=source,
            dst_ref=target.at[place],
            send_sem=send_sem.at[which],
            recv_sem=recv_sem.at[which],
            device_id={axis: other},
            device_id_type=MESH,
        ).start()

    side = math.isqrt(nc // 2)
    core = lax.rem(ctx_pos, 2)
    chip_row, chip_column = ctx_pos // (2 * side), lax.rem(ctx_pos // 2, side)
    hops = sorted(
        ((i, j) for i in range(side) for j in range(side)),
        key=lambda hop: -around(hop[0], side) - around(hop[1], side),
    )

    def send_to_core(which_core, source, target, which):
        for down, along in hops:
            chip = lax.rem(chip_row + down, side) * side + lax.rem(chip_column + along, side)
            other = 2 * chip + which_core
            if (down, along) == (0, 0):

                @pl.when(core != which_core)
                def _():
                    send("ctx", ctx_pos, other, source(other), target, which)

            else:
                send("ctx", ctx_pos, other, source(other), target, which)

    def arrival(axis, place, count, target, which):
        return pltpu.make_async_remote_copy(
            src_ref=target.at[pl.ds(0, count - 1)],
            dst_ref=target.at[pl.ds(0, count - 1)],
            send_sem=send_sem.at[which],
            recv_sem=recv_sem.at[which],
            device_id={axis: lax.rem(place + 1, count)},
            device_id_type=MESH,
        )

    loads[6].wait()
    starts = []
    running = jnp.int32(0)
    for r in range(lengths.shape[0]):
        starts.append(running)
        running = running + lengths[r]

    def request_at(position):
        total = jnp.zeros(position.shape, F32)
        for start in starts:
            total = total + jnp.where(position >= start, 1.0, 0.0)
        return total

    chunk_first = ctx_pos * tokens + iota((chunks, CHUNK), 0) * CHUNK
    request = request_at(chunk_first + iota((chunks, CHUNK), 1))
    request_end = request_at(chunk_first + (CHUNK - 1))
    request_prior = request_at(chunk_first - 1)
    live_end = jnp.where(request == request_end, 1.0, 0.0)
    live_start = jnp.where(request == request_prior, 1.0, 0.0)
    requests[...] = request

    row = iota((CHUNK, lanes), 0)
    row = jnp.where(row >= HALF, row - HALF, row)
    head_of_lane = iota((CHUNK, lanes), 1) // width
    for kind in range(KINDS):
        spread[kind] = jnp.where(row == kind * ROWS + head_of_lane, 1.0, 0.0).astype(BF16)
    spread_request[...] = jnp.where(iota((CHUNK, CHUNK), 0) == REQUEST_ROW, 1.0, 0.0).astype(BF16)

    loads[0].wait()
    upper = jnp.where(iota((CHUNK, CHUNK), 0) <= iota((CHUNK, CHUNK), 1), 1.0, 0.0)
    stacked = jnp.concatenate([decay[:, k * CHUNK : (k + 1) * CHUNK] for k in range(chunks)], axis=0)
    cum = jnp.dot(stacked, upper, preferred_element_type=F32, precision=lax.Precision.HIGHEST)
    before = jnp.ones((ROWS, CHUNK), F32)
    for k in range(chunks):
        part = cum[k * ROWS : (k + 1) * ROWS]
        middle = jnp.broadcast_to(part[:, HALF - 1 : HALF], part.shape)
        end = jnp.broadcast_to(part[:, CHUNK - 1 :], part.shape)
        from_start = jnp.exp(part) * live_start[k : k + 1]
        factors = [
            jnp.exp(end - part) * live_end[k : k + 1],
            jnp.exp(middle - part),
            jnp.exp(part - middle),
            from_start,
            from_start * before,
        ]
        before = before * jnp.broadcast_to(from_start[:, CHUNK - 1 :], part.shape)
        values = jnp.concatenate(factors, axis=0)
        high = values.astype(BF16).astype(F32)
        request_rows = jnp.broadcast_to(request[k : k + 1], (ROWS, CHUNK))
        blank = jnp.zeros((HALF - REQUEST_ROW - ROWS, CHUNK), F32)
        blank_low = jnp.zeros((HALF - REQUEST_ROW, CHUNK), F32)
        whole = jnp.concatenate([high, request_rows, blank, values - high, blank_low], axis=0)
        table[k] = whole.T.astype(BF16)
    decay_out[...] = table[chunks - 1, CHUNK - 16 :, :].astype(F32)[15:16]
    leaving[...] = matmul(table[:, CHUNK - 16 :, :].reshape(16 * chunks, CHUNK), spread[FROM_CHUNK])

    loads[1].wait()
    for k in range(chunks):
        b_turned[k] = b[k * CHUNK : (k + 1) * CHUNK, :].T
    loads[2].wait()
    for half in range(2):
        part = slice(half * share, (half + 1) * share)
        entering = jnp.zeros((state_size, share), F32)
        for k in range(chunks):
            rows = slice(k * CHUNK, (k + 1) * CHUNK)
            local_state[k, :, part] = entering.astype(BF16)
            scaled = (x[rows, part].astype(F32) * matmul(table[k], spread[TO_END, :, part])).astype(BF16)
            entering = leaving[16 * k + 15 : 16 * k + 16, part] * entering + matmul(b_turned[k], scaled)
        for i in range(nc // 2):
            slice_out[2 * i + half] = entering[i * share_rows : (i + 1) * share_rows]
        if half == 0:
            pl.semaphore_wait(barrier, nc - 1 + 2)
            if rounds:
                signal_heads(ready.at[0], rounds[0])
            for which_core in range(2):
                send_to_core(which_core, lambda other: decay_out, decay_in, 0)
        send_to_core(half, lambda other: slice_out.at[other], slice_in, 1)
    decay_in[ctx_pos] = decay_out[...]
    slice_in[ctx_pos] = slice_out[ctx_pos]

    def at(k):
        return pl.ds(pl.multiple_of(k * CHUNK, CHUNK), CHUNK)

    loads[3].wait()
    loads[4].wait()
    loads[5].wait()
    lane_head = iota((1, lanes), 1) // width
    skip_row = jnp.zeros((1, lanes), F32)
    for h in range(ROWS):
        skip_row = jnp.where(lane_head == h, skip[h], skip_row)
    causal = iota((CHUNK, CHUNK), 0) >= iota((CHUNK, CHUNK), 1)

    def own_part(k, carry):
        rows = at(k)
        maps = c[rows, :]
        same = matmul(table[k], spread_request[...]) == requests[pl.ds(k, 1), :]
        scores = jnp.where(causal & same, matmul(maps, b_turned[k]), 0.0).astype(BF16)
        wide = x[rows, :].astype(F32)
        keys = (wide * matmul(table[k], spread[TO_KEY])).astype(BF16)
        total = matmul(scores, keys) * matmul(table[k], spread[TO_QUERY])
        total += matmul(maps, local_state[k]) * matmul(table[k], spread[FROM_CHUNK])
        partial[rows, :] = total + skip_row * wide
        from_device[rows, :] = matmul(table[k], spread[FROM_DEVICE])
        branch = z[rows, :].astype(F32)
        gate[rows, :] = branch / (1.0 + jnp.exp(-branch))
        return carry

    lax.fori_loop(0, chunks, own_part, 0)

    def hear(i):
        pl.semaphore_wait(ready.at[i], 2)
        if i + 1 < len(rounds):
            signal_heads(ready.at[i + 1], rounds[i + 1])

    for i in range(len(rounds))[:1]:
        hear(i)

    for target, which in ((decay_in, 0), (slice_in, 1)):
        arrived = arrival("ctx", ctx_pos, nc, target, which)
        arrived.wait_recv()
        arrived.wait_send()
    rows_in = jnp.concatenate([decay_in[i] for i in range(nc)], axis=0).astype(BF16)
    part = pl.ds(pl.multiple_of(core * share, share), share)
    steps = matmul(rows_in, spread[FROM_DEVICE, :, part])
    entering = jnp.zeros((share_rows, share), F32)
    for i in range(nc):
        enter_out[i] = entering
        entering = steps[i : i + 1] * entering + slice_in[i]
    for which_core in range(2):
        send_to_core(which_core, lambda other: enter_out.at[other], enter_in, 2)
    for i in range(len(rounds))[1:2]:
        hear(i)
    enter_in[ctx_pos] = enter_out[ctx_pos]
    arrived = arrival("ctx", ctx_pos, nc, enter_in, 2)
    arrived.wait_recv()
    for half in range(2):
        for i in range(nc // 2):
            state[i * share_rows : (i + 1) * share_rows, half * share : (half + 1) * share] = enter_in[2 * i + half]
    entered = state[...].astype(BF16)

    step_rows = 2 * CHUNK
    for k in range(tokens // step_rows):
        rows = slice(k * step_rows, (k + 1) * step_rows)
        output = partial[rows, :] + matmul(c[rows, :], entered) * from_device[rows, :]
        gates = output.astype(BF16).astype(F32) * gate[rows, :]
        gated[rows, :] = gates
        squared = gates * gates
        folded = squared[:, :CHUNK]
        for i in range(1, lanes // CHUNK):
            folded = folded + squared[:, i * CHUNK : (i + 1) * CHUNK]
        for i in range(2):
            square_out[2 * k + i : 2 * k + i + 1, :] = jnp.sum(
                folded[i * CHUNK : (i + 1) * CHUNK].T, axis=0, keepdims=True
            )

    for i in range(len(rounds))[2:]:
        hear(i)
    for offset in sorted(range(1, nh), key=lambda offset: -around(offset, nh)):
        send("head", head_pos, lax.rem(head_pos + offset, nh), square_out, square_in, 3)
    square_in[head_pos] = square_out[...]
    arrived.wait_send()
    arrived = arrival("head", head_pos, nh, square_in, 3)
    arrived.wait_recv()
    squares = square_in[0]
    for i in range(1, nh):
        squares = squares + square_in[i]
    scales[...] = lax.rsqrt(squares / (nh * lanes) + EPS)
    arrived.wait_send()


def normalize(gated, scales, gain, out_hbm, out, sem):
    tokens, lanes = gated.shape
    copies = []
    for k in range(tokens // CHUNK):
        rows = slice(k * CHUNK, (k + 1) * CHUNK)
        scale = jnp.broadcast_to(scales[k : k + 1, :], (CHUNK, CHUNK)).T
        scale = jnp.concatenate([scale] * (lanes // CHUNK), axis=1)
        out[rows, :] = (gated[rows, :] * scale * gain[...]).astype(BF16)
        copies.append(pltpu.make_async_copy(out.at[rows, :], out_hbm.at[rows, :], sem.at[k]))
        copies[-1].start()
    for copy in copies:
        copy.wait()


def on_device(nh, nc, head_inputs, gate_z, input_b, output_c, log_decay, lengths, skip_coef, norm_gain):
    tokens, lanes = head_inputs.shape
    heads = skip_coef.shape[0]
    assert heads == ROWS and tokens == ROWS * CHUNK
    state_size = CHUNK
    groups = input_b.shape[1] // state_size
    chunks = tokens // CHUNK
    share = lanes // 2
    share_rows = 2 * state_size // nc
    vmem, smem, hbm = pltpu.VMEM, pltpu.SMEM, pltpu.HBM
    gated, scales = pl.pallas_call(
        functools.partial(kernel, nh, nc, heads * nh // groups),
        out_shape=(
            jax.ShapeDtypeStruct((tokens, lanes), F32),
            jax.ShapeDtypeStruct((chunks, CHUNK), F32),
        ),
        in_specs=[pl.BlockSpec(memory_space=hbm)] * 7,
        out_specs=(pl.BlockSpec(memory_space=vmem), pl.BlockSpec(memory_space=vmem)),
        scratch_shapes=[
            smem(lengths.shape, jnp.int32),
            smem(skip_coef.shape, F32),
            vmem((tokens, lanes), BF16),
            vmem((tokens, lanes), BF16),
            vmem((tokens, state_size), BF16),
            vmem((tokens, state_size), BF16),
            vmem((chunks, state_size, CHUNK), BF16),
            vmem((heads, tokens), F32),
            vmem((chunks, CHUNK, CHUNK), BF16),
            vmem((KINDS, CHUNK, lanes), BF16),
            vmem((CHUNK, CHUNK), BF16),
            vmem((chunks, CHUNK), F32),
            vmem((16 * chunks, lanes), F32),
            vmem((chunks, state_size, lanes), BF16),
            vmem((state_size, lanes), F32),
            vmem((tokens, lanes), F32),
            vmem((tokens, lanes), F32),
            vmem((tokens, lanes), F32),
            vmem((1, CHUNK), F32),
            vmem((nc, 1, CHUNK), F32),
            vmem((nc, share_rows, share), F32),
            vmem((nc, share_rows, share), F32),
            vmem((nc, share_rows, share), F32),
            vmem((nc, share_rows, share), F32),
            vmem((chunks, CHUNK), F32),
            vmem((nh, chunks, CHUNK), F32),
            pltpu.SemaphoreType.DMA((7,)),
            pltpu.SemaphoreType.DMA((4,)),
            pltpu.SemaphoreType.DMA((4,)),
            pltpu.SemaphoreType.REGULAR((4,)),
        ],
        compiler_params=pltpu.CompilerParams(
            collective_id=0, has_side_effects=True, vmem_limit_bytes=24 << 20
        ),
    )(*(
        pltpu.with_memory_space_constraint(operand, hbm)
        for operand in (lengths, skip_coef, head_inputs, gate_z, input_b, output_c, log_decay.T)
    ))
    return pl.pallas_call(
        normalize,
        out_shape=jax.ShapeDtypeStruct((tokens, lanes), BF16),
        in_specs=[pl.BlockSpec(memory_space=vmem)] * 3,
        out_specs=pl.BlockSpec(memory_space=hbm),
        scratch_shapes=[vmem((tokens, lanes), BF16), pltpu.SemaphoreType.DMA((chunks,))],
        compiler_params=pltpu.CompilerParams(vmem_limit_bytes=8 << 20),
    )(gated, scales, norm_gain.reshape(1, lanes))


def solution(mesh):
    return jax.shard_map(
        functools.partial(on_device, mesh.shape["head"], mesh.shape["ctx"]),
        mesh=mesh,
        in_specs=(
            P("ctx", "head"),
            P("ctx", "head"),
            P("ctx", None),
            P("ctx", None),
            P("ctx", "head"),
            P(),
            P("head"),
            P("head"),
        ),
        out_specs=P("ctx", "head"),
        check_vma=False,
    )
```

```python
import functools
import math

import jax
import jax.numpy as jnp
from jax import lax
from jax.experimental import pallas as pl
from jax.experimental.pallas import tpu as pltpu
from jax.sharding import PartitionSpec as P

MESH = pl.DeviceIdType.MESH
CHUNK = 128
HALF = CHUNK // 2
ROWS = 8
EPS = 1e-05
TO_END, TO_KEY, TO_QUERY, FROM_CHUNK, FROM_DEVICE = range(5)
KINDS = 5
REQUEST_ROW = KINDS * ROWS
F32, BF16 = jnp.float32, jnp.bfloat16


def iota(shape, dim):
    return lax.broadcasted_iota(jnp.int32, shape, dim)


def matmul(left, right):
    return jnp.dot(left, right, preferred_element_type=F32)


def around(offset, count):
    return min(offset, count - offset)


def kernel(
    nh, nc, group_heads, lengths_hbm, skip_hbm, x_hbm, z_hbm, b_hbm, c_hbm, decay_hbm, gated, scales,
    lengths, skip, x, z, b, c, b_turned, decay, table, spread, spread_request, requests, leaving, local_state, state,
    partial, gate, from_device, decay_out, decay_in, slice_out, slice_in, enter_out, enter_in,
    square_out, square_in, load_sem, send_sem, recv_sem, ready,
):
    head_pos = lax.axis_index("head")
    ctx_pos = lax.axis_index("ctx")
    tokens, lanes = x.shape
    chunks = tokens // CHUNK
    width = lanes // ROWS
    state_size = b.shape[1]
    share_rows, share = slice_in.shape[1:]
    group = head_pos * ROWS // group_heads
    columns = pl.ds(pl.multiple_of(group * state_size, state_size), state_size)
    loads = [
        pltpu.make_async_copy(decay_hbm, decay, load_sem.at[0]),
        pltpu.make_async_copy(b_hbm.at[:, columns], b, load_sem.at[1]),
        pltpu.make_async_copy(x_hbm, x, load_sem.at[2]),
        pltpu.make_async_copy(c_hbm.at[:, columns], c, load_sem.at[3]),
        pltpu.make_async_copy(z_hbm, z, load_sem.at[4]),
        pltpu.make_async_copy(skip_hbm, skip, load_sem.at[5]),
        pltpu.make_async_copy(lengths_hbm, lengths, load_sem.at[6]),
    ]
    for i in (6, 0, 1, 2, 3, 4, 5):
        loads[i].start()

    barrier = pltpu.get_barrier_semaphore()

    def greet(step, carry):
        other = lax.rem(ctx_pos + step, nc)
        pl.semaphore_signal(barrier, inc=1, device_id={"ctx": other}, device_id_type=MESH)
        return carry

    def signal_heads(semaphore, distance):
        for offset in (distance, nh - distance):
            pl.semaphore_signal(
                semaphore, inc=1, device_id={"head": lax.rem(head_pos + offset, nh)}, device_id_type=MESH
            )

    lax.fori_loop(1, nc, greet, 0)
    signal_heads(barrier, 1)
    rounds = [2**i for i in range(nh.bit_length()) if 2 * 2**i < nh]

    def send(axis, place, other, source, target, which):
        pltpu.make_async_remote_copy(
            src_ref=source,
            dst_ref=target.at[place],
            send_sem=send_sem.at[which],
            recv_sem=recv_sem.at[which],
            device_id={axis: other},
            device_id_type=MESH,
        ).start()

    side = math.isqrt(nc // 2)
    core = lax.rem(ctx_pos, 2)
    chip_row, chip_column = ctx_pos // (2 * side), lax.rem(ctx_pos // 2, side)
    hops = sorted(
        ((i, j) for i in range(side) for j in range(side)),
        key=lambda hop: -around(hop[0], side) - around(hop[1], side),
    )

    def send_to_core(which_core, source, target, which, first_too=True):
        for down, along in hops:
            chip = lax.rem(chip_row + down, side) * side + lax.rem(chip_column + along, side)
            other = 2 * chip + which_core
            wanted = True if first_too else chip != 0
            if (down, along) == (0, 0):
                wanted &= core != which_core

            def one(other=other):
                send("ctx", ctx_pos, other, source(other), target, which)

            if wanted is True:
                one()
            else:
                pl.when(wanted)(one)

    def arrival(axis, place, count, target, which):
        return pltpu.make_async_remote_copy(
            src_ref=target.at[pl.ds(0, count - 1)],
            dst_ref=target.at[pl.ds(0, count - 1)],
            send_sem=send_sem.at[which],
            recv_sem=recv_sem.at[which],
            device_id={axis: lax.rem(place + 1, count)},
            device_id_type=MESH,
        )

    loads[6].wait()
    starts = []
    running = jnp.int32(0)
    for r in range(lengths.shape[0]):
        starts.append(running)
        running = running + lengths[r]

    def request_at(position):
        total = jnp.zeros(position.shape, F32)
        for start in starts:
            total = total + jnp.where(position >= start, 1.0, 0.0)
        return total

    chunk_first = ctx_pos * tokens + iota((chunks, CHUNK), 0) * CHUNK
    request = request_at(chunk_first + iota((chunks, CHUNK), 1))
    request_end = request_at(chunk_first + (CHUNK - 1))
    request_prior = request_at(chunk_first - 1)
    live_end = jnp.where(request == request_end, 1.0, 0.0)
    live_start = jnp.where(request == request_prior, 1.0, 0.0)
    requests[...] = request

    row = iota((CHUNK, lanes), 0)
    row = jnp.where(row >= HALF, row - HALF, row)
    head_of_lane = iota((CHUNK, lanes), 1) // width
    for kind in range(KINDS):
        spread[kind] = jnp.where(row == kind * ROWS + head_of_lane, 1.0, 0.0).astype(BF16)
    spread_request[...] = jnp.where(iota((CHUNK, CHUNK), 0) == REQUEST_ROW, 1.0, 0.0).astype(BF16)

    loads[0].wait()
    upper = jnp.where(iota((CHUNK, CHUNK), 0) <= iota((CHUNK, CHUNK), 1), 1.0, 0.0)
    stacked = jnp.concatenate([decay[:, k * CHUNK : (k + 1) * CHUNK] for k in range(chunks)], axis=0)
    cum = jnp.dot(stacked, upper, preferred_element_type=F32, precision=lax.Precision.HIGHEST)
    before = jnp.ones((ROWS, CHUNK), F32)
    for k in range(chunks):
        part = cum[k * ROWS : (k + 1) * ROWS]
        middle = jnp.broadcast_to(part[:, HALF - 1 : HALF], part.shape)
        end = jnp.broadcast_to(part[:, CHUNK - 1 :], part.shape)
        from_start = jnp.exp(part) * live_start[k : k + 1]
        factors = [
            jnp.exp(end - part) * live_end[k : k + 1],
            jnp.exp(middle - part),
            jnp.exp(part - middle),
            from_start,
            from_start * before,
        ]
        before = before * jnp.broadcast_to(from_start[:, CHUNK - 1 :], part.shape)
        values = jnp.concatenate(factors, axis=0)
        high = values.astype(BF16).astype(F32)
        request_rows = jnp.broadcast_to(request[k : k + 1], (ROWS, CHUNK))
        blank = jnp.zeros((HALF - REQUEST_ROW - ROWS, CHUNK), F32)
        blank_low = jnp.zeros((HALF - REQUEST_ROW, CHUNK), F32)
        whole = jnp.concatenate([high, request_rows, blank, values - high, blank_low], axis=0)
        table[k] = whole.T.astype(BF16)
    decay_out[...] = table[chunks - 1, CHUNK - 16 :, :].astype(F32)[15:16]
    leaving[...] = matmul(table[:, CHUNK - 16 :, :].reshape(16 * chunks, CHUNK), spread[FROM_CHUNK])

    loads[1].wait()
    for k in range(chunks):
        b_turned[k] = b[k * CHUNK : (k + 1) * CHUNK, :].T
    loads[2].wait()
    for half in range(2):
        part = slice(half * share, (half + 1) * share)
        entering = jnp.zeros((state_size, share), F32)
        for k in range(chunks):
            rows = slice(k * CHUNK, (k + 1) * CHUNK)
            local_state[k, :, part] = entering.astype(BF16)
            scaled = (x[rows, part].astype(F32) * matmul(table[k], spread[TO_END, :, part])).astype(BF16)
            entering = leaving[16 * k + 15 : 16 * k + 16, part] * entering + matmul(b_turned[k], scaled)
        for i in range(nc // 2):
            slice_out[2 * i + half] = entering[i * share_rows : (i + 1) * share_rows]
        if half == 0:
            pl.semaphore_wait(barrier, nc - 1 + 2)
            if rounds:
                signal_heads(ready.at[0], rounds[0])
            for which_core in range(2):
                send_to_core(which_core, lambda other: decay_out, decay_in, 0)
        send_to_core(half, lambda other: slice_out.at[other], slice_in, 1)
    first_copy = pltpu.make_async_remote_copy(
        src_ref=slice_out,
        dst_ref=enter_in,
        send_sem=send_sem.at[4],
        recv_sem=recv_sem.at[4],
        device_id={"ctx": 1 - core},
        device_id_type=MESH,
    )
    pl.when(ctx_pos == 0)(first_copy.start)
    decay_in[ctx_pos] = decay_out[...]
    slice_in[ctx_pos] = slice_out[ctx_pos]

    def at(k):
        return pl.ds(pl.multiple_of(k * CHUNK, CHUNK), CHUNK)

    loads[3].wait()
    loads[4].wait()
    loads[5].wait()
    lane_head = iota((1, lanes), 1) // width
    skip_row = jnp.zeros((1, lanes), F32)
    for h in range(ROWS):
        skip_row = jnp.where(lane_head == h, skip[h], skip_row)
    causal = iota((CHUNK, CHUNK), 0) >= iota((CHUNK, CHUNK), 1)

    def own_part(k, carry):
        rows = at(k)
        maps = c[rows, :]
        same = matmul(table[k], spread_request[...]) == requests[pl.ds(k, 1), :]
        scores = jnp.where(causal & same, matmul(maps, b_turned[k]), 0.0).astype(BF16)
        wide = x[rows, :].astype(F32)
        keys = (wide * matmul(table[k], spread[TO_KEY])).astype(BF16)
        total = matmul(scores, keys) * matmul(table[k], spread[TO_QUERY])
        total += matmul(maps, local_state[k]) * matmul(table[k], spread[FROM_CHUNK])
        partial[rows, :] = total + skip_row * wide
        from_device[rows, :] = matmul(table[k], spread[FROM_DEVICE])
        branch = z[rows, :].astype(F32)
        gate[rows, :] = branch / (1.0 + jnp.exp(-branch))
        return carry

    lax.fori_loop(0, chunks, own_part, 0)

    def hear(i):
        pl.semaphore_wait(ready.at[i], 2)
        if i + 1 < len(rounds):
            signal_heads(ready.at[i + 1], rounds[i + 1])

    for i in range(len(rounds))[:1]:
        hear(i)

    for target, which in ((decay_in, 0), (slice_in, 1)):
        arrived = arrival("ctx", ctx_pos, nc, target, which)
        arrived.wait_recv()
        arrived.wait_send()
    rows_in = jnp.concatenate([decay_in[i] for i in range(nc)], axis=0).astype(BF16)
    part = pl.ds(pl.multiple_of(core * share, share), share)
    steps = matmul(rows_in, spread[FROM_DEVICE, :, part])
    entering = jnp.zeros((share_rows, share), F32)
    for i in range(nc):
        enter_out[i] = entering
        entering = steps[i : i + 1] * entering + slice_in[i]
    for which_core in range(2):
        send_to_core(which_core, lambda other: enter_out.at[other], enter_in, 2, first_too=False)
    for i in range(len(rounds))[1:2]:
        hear(i)
    arrived = arrival("ctx", ctx_pos, nc, enter_in, 2)

    @pl.when(ctx_pos == 0)
    def _():
        enter_in[...] = jnp.zeros(enter_in.shape, F32)

    @pl.when(ctx_pos == 1)
    def _():
        first_copy.wait_recv()

    @pl.when(ctx_pos >= 2)
    def _():
        enter_in[ctx_pos] = enter_out[ctx_pos]
        arrived.wait_recv()

    for half in range(2):
        for i in range(nc // 2):
            state[i * share_rows : (i + 1) * share_rows, half * share : (half + 1) * share] = enter_in[2 * i + half]
    entered = state[...].astype(BF16)

    step_rows = 2 * CHUNK
    for k in range(tokens // step_rows):
        rows = slice(k * step_rows, (k + 1) * step_rows)
        output = partial[rows, :] + matmul(c[rows, :], entered) * from_device[rows, :]
        gates = output.astype(BF16).astype(F32) * gate[rows, :]
        gated[rows, :] = gates
        squared = gates * gates
        folded = squared[:, :CHUNK]
        for i in range(1, lanes // CHUNK):
            folded = folded + squared[:, i * CHUNK : (i + 1) * CHUNK]
        for i in range(2):
            square_out[2 * k + i : 2 * k + i + 1, :] = jnp.sum(
                folded[i * CHUNK : (i + 1) * CHUNK].T, axis=0, keepdims=True
            )

    for i in range(len(rounds))[2:]:
        hear(i)
    for offset in sorted(range(1, nh), key=lambda offset: -around(offset, nh)):
        send("head", head_pos, lax.rem(head_pos + offset, nh), square_out, square_in, 3)
    square_in[head_pos] = square_out[...]
    sent = pltpu.make_async_remote_copy(
        src_ref=enter_out.at[pl.ds(0, nc - 3)],
        dst_ref=enter_out.at[pl.ds(0, nc - 3)],
        send_sem=send_sem.at[2],
        recv_sem=recv_sem.at[2],
        device_id={"ctx": 1 - core},
        device_id_type=MESH,
    )

    @pl.when(ctx_pos == 0)
    def _():
        first_copy.wait_send()

    sent.wait_send()

    @pl.when(ctx_pos < 2)
    def _():
        pltpu.make_async_remote_copy(
            src_ref=enter_out.at[0],
            dst_ref=enter_out.at[0],
            send_sem=send_sem.at[2],
            recv_sem=recv_sem.at[2],
            device_id={"ctx": 1 - core},
            device_id_type=MESH,
        ).wait_send()

    arrived = arrival("head", head_pos, nh, square_in, 3)
    arrived.wait_recv()
    squares = square_in[0]
    for i in range(1, nh):
        squares = squares + square_in[i]
    scales[...] = lax.rsqrt(squares / (nh * lanes) + EPS)
    arrived.wait_send()


def normalize(gated, scales, gain, out_hbm, out, sem):
    tokens, lanes = gated.shape
    copies = []
    for k in range(tokens // CHUNK):
        rows = slice(k * CHUNK, (k + 1) * CHUNK)
        scale = jnp.broadcast_to(scales[k : k + 1, :], (CHUNK, CHUNK)).T
        scale = jnp.concatenate([scale] * (lanes // CHUNK), axis=1)
        out[rows, :] = (gated[rows, :] * scale * gain[...]).astype(BF16)
        copies.append(pltpu.make_async_copy(out.at[rows, :], out_hbm.at[rows, :], sem.at[k]))
        copies[-1].start()
    for copy in copies:
        copy.wait()


def on_device(nh, nc, head_inputs, gate_z, input_b, output_c, log_decay, lengths, skip_coef, norm_gain):
    tokens, lanes = head_inputs.shape
    heads = skip_coef.shape[0]
    assert heads == ROWS and tokens == ROWS * CHUNK
    state_size = CHUNK
    groups = input_b.shape[1] // state_size
    chunks = tokens // CHUNK
    share = lanes // 2
    share_rows = 2 * state_size // nc
    vmem, smem, hbm = pltpu.VMEM, pltpu.SMEM, pltpu.HBM
    gated, scales = pl.pallas_call(
        functools.partial(kernel, nh, nc, heads * nh // groups),
        out_shape=(
            jax.ShapeDtypeStruct((tokens, lanes), F32),
            jax.ShapeDtypeStruct((chunks, CHUNK), F32),
        ),
        in_specs=[pl.BlockSpec(memory_space=hbm)] * 7,
        out_specs=(pl.BlockSpec(memory_space=vmem), pl.BlockSpec(memory_space=vmem)),
        scratch_shapes=[
            smem(lengths.shape, jnp.int32),
            smem(skip_coef.shape, F32),
            vmem((tokens, lanes), BF16),
            vmem((tokens, lanes), BF16),
            vmem((tokens, state_size), BF16),
            vmem((tokens, state_size), BF16),
            vmem((chunks, state_size, CHUNK), BF16),
            vmem((heads, tokens), F32),
            vmem((chunks, CHUNK, CHUNK), BF16),
            vmem((KINDS, CHUNK, lanes), BF16),
            vmem((CHUNK, CHUNK), BF16),
            vmem((chunks, CHUNK), F32),
            vmem((16 * chunks, lanes), F32),
            vmem((chunks, state_size, lanes), BF16),
            vmem((state_size, lanes), F32),
            vmem((tokens, lanes), F32),
            vmem((tokens, lanes), F32),
            vmem((tokens, lanes), F32),
            vmem((1, CHUNK), F32),
            vmem((nc, 1, CHUNK), F32),
            vmem((nc, share_rows, share), F32),
            vmem((nc, share_rows, share), F32),
            vmem((nc, share_rows, share), F32),
            vmem((nc, share_rows, share), F32),
            vmem((chunks, CHUNK), F32),
            vmem((nh, chunks, CHUNK), F32),
            pltpu.SemaphoreType.DMA((7,)),
            pltpu.SemaphoreType.DMA((5,)),
            pltpu.SemaphoreType.DMA((5,)),
            pltpu.SemaphoreType.REGULAR((4,)),
        ],
        compiler_params=pltpu.CompilerParams(
            collective_id=0, has_side_effects=True, vmem_limit_bytes=24 << 20
        ),
    )(*(
        pltpu.with_memory_space_constraint(operand, hbm)
        for operand in (lengths, skip_coef, head_inputs, gate_z, input_b, output_c, log_decay.T)
    ))
    return pl.pallas_call(
        normalize,
        out_shape=jax.ShapeDtypeStruct((tokens, lanes), BF16),
        in_specs=[pl.BlockSpec(memory_space=vmem)] * 3,
        out_specs=pl.BlockSpec(memory_space=hbm),
        scratch_shapes=[vmem((tokens, lanes), BF16), pltpu.SemaphoreType.DMA((chunks,))],
        compiler_params=pltpu.CompilerParams(vmem_limit_bytes=8 << 20),
    )(gated, scales, norm_gain.reshape(1, lanes))


def solution(mesh):
    return jax.shard_map(
        functools.partial(on_device, mesh.shape["head"], mesh.shape["ctx"]),
        mesh=mesh,
        in_specs=(
            P("ctx", "head"),
            P("ctx", "head"),
            P("ctx", None),
            P("ctx", None),
            P("ctx", "head"),
            P(),
            P("head"),
            P("head"),
        ),
        out_specs=P("ctx", "head"),
        check_vma=False,
    )
```

```python
import functools
import math

import jax
import jax.numpy as jnp
from jax import lax
from jax.experimental import pallas as pl
from jax.experimental.pallas import tpu as pltpu
from jax.sharding import PartitionSpec as P

MESH = pl.DeviceIdType.MESH
CHUNK = 128
HALF = CHUNK // 2
ROWS = 8
EPS = 1e-05
TO_END, TO_KEY, TO_QUERY, FROM_CHUNK, FROM_DEVICE = range(5)
KINDS = 5
REQUEST_ROW = KINDS * ROWS
DECAY, FIRST_HALF, SECOND_HALF, STEP_BEFORE, SLICE_BEFORE, STEP, SLICE, ENTER, SWAP, SQUARE = range(10)
F32, BF16 = jnp.float32, jnp.bfloat16


def iota(shape, dim):
    return lax.broadcasted_iota(jnp.int32, shape, dim)


def matmul(left, right):
    return jnp.dot(left, right, preferred_element_type=F32)


def around(offset, count):
    return min(offset, count - offset)


def kernel(
    nh, nc, group_heads, lengths_hbm, skip_hbm, x_hbm, z_hbm, b_hbm, c_hbm, decay_hbm, gated, scales,
    lengths, skip, x, z, b, c, b_turned, decay, table, spread, spread_request, requests, leaving, local_state, state,
    partial, gate, from_device, decay_out, decay_in, decays, state_out, state_in, step_out, step_in,
    slice_out, slice_in, enter_out, enter_in, enter_other, square_out, square_in,
    load_sem, send_sem, recv_sem, ready,
):
    head_pos = lax.axis_index("head")
    ctx_pos = lax.axis_index("ctx")
    tokens, lanes = x.shape
    chunks = tokens // CHUNK
    width = lanes // ROWS
    state_size = b.shape[1]
    share_rows, share = slice_in.shape[1:]
    group = head_pos * ROWS // group_heads
    columns = pl.ds(pl.multiple_of(group * state_size, state_size), state_size)
    loads = [
        pltpu.make_async_copy(decay_hbm, decay, load_sem.at[0]),
        pltpu.make_async_copy(b_hbm.at[:, columns], b, load_sem.at[1]),
        pltpu.make_async_copy(x_hbm, x, load_sem.at[2]),
        pltpu.make_async_copy(c_hbm.at[:, columns], c, load_sem.at[3]),
        pltpu.make_async_copy(z_hbm, z, load_sem.at[4]),
        pltpu.make_async_copy(skip_hbm, skip, load_sem.at[5]),
        pltpu.make_async_copy(lengths_hbm, lengths, load_sem.at[6]),
    ]
    for i in (6, 0, 1, 2, 3, 4, 5):
        loads[i].start()

    barrier = pltpu.get_barrier_semaphore()

    side = math.isqrt(nc // 2)
    core = lax.rem(ctx_pos, 2)
    chip = ctx_pos // 2
    chip_row, chip_column = chip // side, lax.rem(chip, side)
    not_first_row, not_last_row = chip_row > 0, chip_row < side - 1

    def device_at(down, along):
        return (lax.rem(chip_row + down, side) * side + lax.rem(chip_column + along, side)) * 2 + core

    def signal_ctx(other):
        pl.semaphore_signal(barrier, inc=1, device_id={"ctx": other}, device_id_type=MESH)

    def signal_heads(semaphore, distance):
        for offset in (distance, nh - distance):
            pl.semaphore_signal(
                semaphore, inc=1, device_id={"head": lax.rem(head_pos + offset, nh)}, device_id_type=MESH
            )

    signal_ctx(ctx_pos + 1 - 2 * core)
    for along in range(1, side):
        signal_ctx(device_at(0, along))
    for along in range(side):
        signal_ctx(device_at(side - 1, along))
    signal_heads(barrier, 1)
    rounds = [2**i for i in range(nh.bit_length()) if 2 * 2**i < nh]

    waits = []

    def send(device, source, target, which, condition=None):
        copy = pltpu.make_async_remote_copy(
            src_ref=source,
            dst_ref=target,
            send_sem=send_sem.at[len(waits)],
            recv_sem=recv_sem.at[which],
            device_id=device,
            device_id_type=MESH,
        )
        waits.append((copy, condition))
        if condition is None:
            copy.start()
        else:
            pl.when(condition)(copy.start)

    def await_bytes(buffer, which):
        pltpu.make_async_remote_copy(
            src_ref=buffer,
            dst_ref=buffer,
            send_sem=send_sem.at[0],
            recv_sem=recv_sem.at[which],
            device_id={"ctx": ctx_pos + 1 - 2 * core},
            device_id_type=MESH,
        ).wait_recv()

    twin = {"ctx": ctx_pos + 1 - 2 * core}

    loads[6].wait()
    starts = []
    running = jnp.int32(0)
    for r in range(lengths.shape[0]):
        starts.append(running)
        running = running + lengths[r]

    def request_at(position):
        total = jnp.zeros(position.shape, F32)
        for start in starts:
            total = total + jnp.where(position >= start, 1.0, 0.0)
        return total

    chunk_first = ctx_pos * tokens + iota((chunks, CHUNK), 0) * CHUNK
    request = request_at(chunk_first + iota((chunks, CHUNK), 1))
    request_end = request_at(chunk_first + (CHUNK - 1))
    request_prior = request_at(chunk_first - 1)
    live_end = jnp.where(request == request_end, 1.0, 0.0)
    live_start = jnp.where(request == request_prior, 1.0, 0.0)
    requests[...] = request

    row = iota((CHUNK, lanes), 0)
    row = jnp.where(row >= HALF, row - HALF, row)
    head_of_lane = iota((CHUNK, lanes), 1) // width
    for kind in range(KINDS):
        spread[kind] = jnp.where(row == kind * ROWS + head_of_lane, 1.0, 0.0).astype(BF16)
    spread_request[...] = jnp.where(iota((CHUNK, CHUNK), 0) == REQUEST_ROW, 1.0, 0.0).astype(BF16)

    loads[0].wait()
    upper = jnp.where(iota((CHUNK, CHUNK), 0) <= iota((CHUNK, CHUNK), 1), 1.0, 0.0)
    stacked = jnp.concatenate([decay[:, k * CHUNK : (k + 1) * CHUNK] for k in range(chunks)], axis=0)
    cum = jnp.dot(stacked, upper, preferred_element_type=F32, precision=lax.Precision.HIGHEST)
    before = jnp.ones((ROWS, CHUNK), F32)
    for k in range(chunks):
        part = cum[k * ROWS : (k + 1) * ROWS]
        middle = jnp.broadcast_to(part[:, HALF - 1 : HALF], part.shape)
        end = jnp.broadcast_to(part[:, CHUNK - 1 :], part.shape)
        from_start = jnp.exp(part) * live_start[k : k + 1]
        factors = [
            jnp.exp(end - part) * live_end[k : k + 1],
            jnp.exp(middle - part),
            jnp.exp(part - middle),
            from_start,
            from_start * before,
        ]
        before = before * jnp.broadcast_to(from_start[:, CHUNK - 1 :], part.shape)
        values = jnp.concatenate(factors, axis=0)
        high = values.astype(BF16).astype(F32)
        request_rows = jnp.broadcast_to(request[k : k + 1], (ROWS, CHUNK))
        blank = jnp.zeros((HALF - REQUEST_ROW - ROWS, CHUNK), F32)
        blank_low = jnp.zeros((HALF - REQUEST_ROW, CHUNK), F32)
        whole = jnp.concatenate([high, request_rows, blank, values - high, blank_low], axis=0)
        table[k] = whole.T.astype(BF16)
    decay_out[...] = table[chunks - 1, CHUNK - 16 :, :].astype(F32)[15:16]
    leaving[...] = matmul(table[:, CHUNK - 16 :, :].reshape(16 * chunks, CHUNK), spread[FROM_CHUNK])

    loads[1].wait()
    for k in range(chunks):
        b_turned[k] = b[k * CHUNK : (k + 1) * CHUNK, :].T
    loads[2].wait()
    for half in range(2):
        part = slice(half * share, (half + 1) * share)
        entering = jnp.zeros((state_size, share), F32)
        for k in range(chunks):
            rows = slice(k * CHUNK, (k + 1) * CHUNK)
            local_state[k, :, part] = entering.astype(BF16)
            scaled = (x[rows, part].astype(F32) * matmul(table[k], spread[TO_END, :, part])).astype(BF16)
            entering = leaving[16 * k + 15 : 16 * k + 16, part] * entering + matmul(b_turned[k], scaled)
        state_out[half] = entering
        if half == 0:
            pl.semaphore_wait(barrier, 2 * side + 2)
            if rounds:
                signal_heads(ready.at[0], rounds[0])
            send(twin, decay_out, decay_in, DECAY)
        send(twin, state_out.at[half], state_in.at[half], FIRST_HALF + half, None if half == 0 else core == 0)

    await_bytes(decay_in, DECAY)
    both = jnp.concatenate([decay_out[...], decay_in[...]] * (ROWS // 2), axis=0).astype(BF16)
    decays[...] = matmul(both, spread[FROM_DEVICE])
    await_bytes(state_in.at[0], FIRST_HALF)

    @pl.when(core == 1)
    def _():
        await_bytes(state_in.at[1], SECOND_HALF)

    mine = pl.ds(pl.multiple_of(core * share, share), share)
    others = pl.ds(pl.multiple_of((1 - core) * share, share), share)
    first_core = core == 0
    own_state, own_decay = state_out[core], decays[0:1, mine]
    got_state, got_decay = state_in[core], decays[1:2, mine]
    joined = jnp.where(first_core, own_state, got_state) * jnp.where(first_core, got_decay, own_decay)
    joined = joined + jnp.where(first_core, got_state, own_state)
    step_out[...] = own_decay * got_decay
    for i in range(side):
        slice_out[i] = joined[i * share_rows : (i + 1) * share_rows]
    for along in range(side):
        other = device_at(1, along)
        column = lax.rem(chip_column + along, side)
        send({"ctx": other}, step_out, step_in.at[chip_column], STEP_BEFORE, not_last_row)
        send({"ctx": other}, slice_out.at[column], slice_in.at[chip_column], SLICE_BEFORE, not_last_row)
    for along in range(1, side):
        other = device_at(0, along)
        column = lax.rem(chip_column + along, side)
        send({"ctx": other}, step_out, step_in.at[side + chip_column], STEP)
        send({"ctx": other}, slice_out.at[column], slice_in.at[side + chip_column], SLICE)
    step_in[side + chip_column] = step_out[...]
    slice_in[side + chip_column] = slice_out[chip_column]

    @pl.when(chip_row == 0)
    def _():
        step_in[0:side] = jnp.zeros((side, 1, share), F32)
        slice_in[0:side] = jnp.zeros((side, share_rows, share), F32)

    def at(k):
        return pl.ds(pl.multiple_of(k * CHUNK, CHUNK), CHUNK)

    loads[3].wait()
    loads[4].wait()
    loads[5].wait()
    lane_head = iota((1, lanes), 1) // width
    skip_row = jnp.zeros((1, lanes), F32)
    for h in range(ROWS):
        skip_row = jnp.where(lane_head == h, skip[h], skip_row)
    causal = iota((CHUNK, CHUNK), 0) >= iota((CHUNK, CHUNK), 1)

    def own_part(k, carry):
        rows = at(k)
        maps = c[rows, :]
        same = matmul(table[k], spread_request[...]) == requests[pl.ds(k, 1), :]
        scores = jnp.where(causal & same, matmul(maps, b_turned[k]), 0.0).astype(BF16)
        wide = x[rows, :].astype(F32)
        keys = (wide * matmul(table[k], spread[TO_KEY])).astype(BF16)
        total = matmul(scores, keys) * matmul(table[k], spread[TO_QUERY])
        total += matmul(maps, local_state[k]) * matmul(table[k], spread[FROM_CHUNK])
        partial[rows, :] = total + skip_row * wide
        from_device[rows, :] = matmul(table[k], spread[FROM_DEVICE])
        branch = z[rows, :].astype(F32)
        gate[rows, :] = branch / (1.0 + jnp.exp(-branch))
        return carry

    lax.fori_loop(0, chunks, own_part, 0)

    def hear(i):
        pl.semaphore_wait(ready.at[i], 2)
        if i + 1 < len(rounds):
            signal_heads(ready.at[i + 1], rounds[i + 1])

    for i in range(len(rounds))[:1]:
        hear(i)

    @pl.when(not_first_row)
    def _():
        await_bytes(step_in.at[0:side], STEP_BEFORE)
        await_bytes(slice_in.at[0:side], SLICE_BEFORE)

    await_bytes(step_in.at[0 : side - 1], STEP)
    await_bytes(slice_in.at[0 : side - 1], SLICE)
    entering = slice_in[0]
    for i in range(1, 2 * side):
        if i >= side:
            enter_out[i - side] = entering
        entering = step_in[i] * entering + slice_in[i] if i < 2 * side - 1 else entering
    for along in range(side - 1, 0, -1):
        column = lax.rem(chip_column + along, side)
        send(
            {"ctx": device_at(0, along)}, enter_out.at[column], enter_in.at[chip_column], ENTER,
            not_first_row | (column > 0),
        )
    for i in range(len(rounds))[1:2]:
        hear(i)

    @pl.when(chip > 0)
    def _():
        enter_in[chip_column] = enter_out[chip_column]
        await_bytes(enter_in.at[0 : side - 1], ENTER)

    send(twin, enter_in, enter_other, SWAP, chip > 0)

    @pl.when(chip > 0)
    def _():
        state[:, mine] = enter_in[...].reshape(state_size, share)
        await_bytes(enter_other, SWAP)
        state[:, others] = enter_other[...].reshape(state_size, share)

    @pl.when(chip == 0)
    def _():
        state[...] = jnp.zeros(state.shape, F32)

    @pl.when(core == 1)
    def _():
        before_core = jnp.concatenate([state_in[0], state_in[1]], axis=1)
        state[...] = decays[1:2, :] * state[...] + before_core

    entered = state[...].astype(BF16)

    step_rows = 2 * CHUNK
    for k in range(tokens // step_rows):
        rows = slice(k * step_rows, (k + 1) * step_rows)
        output = partial[rows, :] + matmul(c[rows, :], entered) * from_device[rows, :]
        gates = output.astype(BF16).astype(F32) * gate[rows, :]
        gated[rows, :] = gates
        squared = gates * gates
        folded = squared[:, :CHUNK]
        for i in range(1, lanes // CHUNK):
            folded = folded + squared[:, i * CHUNK : (i + 1) * CHUNK]
        for i in range(2):
            square_out[2 * k + i : 2 * k + i + 1, :] = jnp.sum(
                folded[i * CHUNK : (i + 1) * CHUNK].T, axis=0, keepdims=True
            )

    for i in range(len(rounds))[2:]:
        hear(i)
    for offset in sorted(range(1, nh), key=lambda offset: -around(offset, nh)):
        send({"head": lax.rem(head_pos + offset, nh)}, square_out, square_in.at[head_pos], SQUARE)
    square_in[head_pos] = square_out[...]
    await_bytes(square_in.at[0 : nh - 1], SQUARE)
    squares = square_in[0]
    for i in range(1, nh):
        squares = squares + square_in[i]
    scales[...] = lax.rsqrt(squares / (nh * lanes) + EPS)
    for copy, condition in waits:
        if condition is None:
            copy.wait_send()
        else:
            pl.when(condition)(copy.wait_send)


def normalize(gated, scales, gain, out_hbm, out, sem):
    tokens, lanes = gated.shape
    copies = []
    for k in range(tokens // CHUNK):
        rows = slice(k * CHUNK, (k + 1) * CHUNK)
        scale = jnp.broadcast_to(scales[k : k + 1, :], (CHUNK, CHUNK)).T
        scale = jnp.concatenate([scale] * (lanes // CHUNK), axis=1)
        out[rows, :] = (gated[rows, :] * scale * gain[...]).astype(BF16)
        copies.append(pltpu.make_async_copy(out.at[rows, :], out_hbm.at[rows, :], sem.at[k]))
        copies[-1].start()
    for copy in copies:
        copy.wait()


def on_device(nh, nc, head_inputs, gate_z, input_b, output_c, log_decay, lengths, skip_coef, norm_gain):
    tokens, lanes = head_inputs.shape
    heads = skip_coef.shape[0]
    assert heads == ROWS and tokens == ROWS * CHUNK
    state_size = CHUNK
    groups = input_b.shape[1] // state_size
    chunks = tokens // CHUNK
    share = lanes // 2
    side = math.isqrt(nc // 2)
    share_rows = state_size // side
    vmem, smem, hbm = pltpu.VMEM, pltpu.SMEM, pltpu.HBM
    gated, scales = pl.pallas_call(
        functools.partial(kernel, nh, nc, heads * nh // groups),
        out_shape=(
            jax.ShapeDtypeStruct((tokens, lanes), F32),
            jax.ShapeDtypeStruct((chunks, CHUNK), F32),
        ),
        in_specs=[pl.BlockSpec(memory_space=hbm)] * 7,
        out_specs=(pl.BlockSpec(memory_space=vmem), pl.BlockSpec(memory_space=vmem)),
        scratch_shapes=[
            smem(lengths.shape, jnp.int32),
            smem(skip_coef.shape, F32),
            vmem((tokens, lanes), BF16),
            vmem((tokens, lanes), BF16),
            vmem((tokens, state_size), BF16),
            vmem((tokens, state_size), BF16),
            vmem((chunks, state_size, CHUNK), BF16),
            vmem((heads, tokens), F32),
            vmem((chunks, CHUNK, CHUNK), BF16),
            vmem((KINDS, CHUNK, lanes), BF16),
            vmem((CHUNK, CHUNK), BF16),
            vmem((chunks, CHUNK), F32),
            vmem((16 * chunks, lanes), F32),
            vmem((chunks, state_size, lanes), BF16),
            vmem((state_size, lanes), F32),
            vmem((tokens, lanes), F32),
            vmem((tokens, lanes), F32),
            vmem((tokens, lanes), F32),
            vmem((1, CHUNK), F32),
            vmem((1, CHUNK), F32),
            vmem((heads, lanes), F32),
            vmem((2, state_size, share), F32),
            vmem((2, state_size, share), F32),
            vmem((1, share), F32),
            vmem((2 * side, 1, share), F32),
            vmem((side, share_rows, share), F32),
            vmem((2 * side, share_rows, share), F32),
            vmem((side, share_rows, share), F32),
            vmem((side, share_rows, share), F32),
            vmem((side, share_rows, share), F32),
            vmem((chunks, CHUNK), F32),
            vmem((nh, chunks, CHUNK), F32),
            pltpu.SemaphoreType.DMA((7,)),
            pltpu.SemaphoreType.DMA((6 * side + nh + 4,)),
            pltpu.SemaphoreType.DMA((10,)),
            pltpu.SemaphoreType.REGULAR((4,)),
        ],
        compiler_params=pltpu.CompilerParams(
            collective_id=0, has_side_effects=True, vmem_limit_bytes=24 << 20
        ),
    )(*(
        pltpu.with_memory_space_constraint(operand, hbm)
        for operand in (lengths, skip_coef, head_inputs, gate_z, input_b, output_c, log_decay.T)
    ))
    return pl.pallas_call(
        normalize,
        out_shape=jax.ShapeDtypeStruct((tokens, lanes), BF16),
        in_specs=[pl.BlockSpec(memory_space=vmem)] * 3,
        out_specs=pl.BlockSpec(memory_space=hbm),
        scratch_shapes=[vmem((tokens, lanes), BF16), pltpu.SemaphoreType.DMA((chunks,))],
        compiler_params=pltpu.CompilerParams(vmem_limit_bytes=8 << 20),
    )(gated, scales, norm_gain.reshape(1, lanes))


def solution(mesh):
    return jax.shard_map(
        functools.partial(on_device, mesh.shape["head"], mesh.shape["ctx"]),
        mesh=mesh,
        in_specs=(
            P("ctx", "head"),
            P("ctx", "head"),
            P("ctx", None),
            P("ctx", None),
            P("ctx", "head"),
            P(),
            P("head"),
            P("head"),
        ),
        out_specs=P("ctx", "head"),
        check_vma=False,
    )
```

```python
import functools
import math

import jax
import jax.numpy as jnp
from jax import lax
from jax.experimental import pallas as pl
from jax.experimental.pallas import tpu as pltpu
from jax.sharding import PartitionSpec as P

MESH = pl.DeviceIdType.MESH
CHUNK = 128
HALF = CHUNK // 2
ROWS = 8
EPS = 1e-05
TO_END, TO_KEY, TO_QUERY, FROM_CHUNK, FROM_DEVICE = range(5)
KINDS = 5
REQUEST_ROW = KINDS * ROWS
DECAY, FIRST_HALF, SECOND_HALF, STEP_BEFORE, SLICE_BEFORE, STEP, SLICE, ENTER, SWAP, SQUARE = range(10)
F32, BF16 = jnp.float32, jnp.bfloat16


def iota(shape, dim):
    return lax.broadcasted_iota(jnp.int32, shape, dim)


def matmul(left, right):
    return jnp.dot(left, right, preferred_element_type=F32)


def around(offset, count):
    return min(offset, count - offset)


def kernel(
    nh, nc, group_heads, lengths_hbm, skip_hbm, x_hbm, z_hbm, b_hbm, c_hbm, decay_hbm, gated, scales,
    lengths, skip, x, z, b, c, b_turned, decay, table, spread, spread_request, requests, leaving, local_state, state,
    partial, gate, from_device, decay_out, decay_in, decays, state_out, state_in, step_out, step_in,
    slice_out, slice_in, enter_out, enter_in, enter_other, square_out, square_in,
    load_sem, send_sem, recv_sem, ready,
):
    head_pos = lax.axis_index("head")
    ctx_pos = lax.axis_index("ctx")
    tokens, lanes = x.shape
    chunks = tokens // CHUNK
    width = lanes // ROWS
    state_size = b.shape[1]
    share_rows, share = slice_in.shape[1:]
    group = head_pos * ROWS // group_heads
    columns = pl.ds(pl.multiple_of(group * state_size, state_size), state_size)
    loads = [
        pltpu.make_async_copy(decay_hbm, decay, load_sem.at[0]),
        pltpu.make_async_copy(b_hbm.at[:, columns], b, load_sem.at[1]),
        pltpu.make_async_copy(x_hbm, x, load_sem.at[2]),
        pltpu.make_async_copy(c_hbm.at[:, columns], c, load_sem.at[3]),
        pltpu.make_async_copy(z_hbm, z, load_sem.at[4]),
        pltpu.make_async_copy(skip_hbm, skip, load_sem.at[5]),
        pltpu.make_async_copy(lengths_hbm, lengths, load_sem.at[6]),
    ]
    for i in (6, 0, 1, 2, 3, 4, 5):
        loads[i].start()

    barrier = pltpu.get_barrier_semaphore()

    side = math.isqrt(nc // 2)
    core = lax.rem(ctx_pos, 2)
    chip = ctx_pos // 2
    chip_row, chip_column = chip // side, lax.rem(chip, side)
    not_first_row, not_last_row = chip_row > 0, chip_row < side - 1

    def device_at(down, along):
        return (lax.rem(chip_row + down, side) * side + lax.rem(chip_column + along, side)) * 2 + core

    def signal_ctx(other):
        pl.semaphore_signal(barrier, inc=1, device_id={"ctx": other}, device_id_type=MESH)

    def signal_heads(semaphore, distance):
        for offset in (distance, nh - distance):
            pl.semaphore_signal(
                semaphore, inc=1, device_id={"head": lax.rem(head_pos + offset, nh)}, device_id_type=MESH
            )

    signal_ctx(ctx_pos + 1 - 2 * core)
    for along in range(1, side):
        signal_ctx(device_at(0, along))
    for along in range(side):
        signal_ctx(device_at(side - 1, along))
    signal_heads(barrier, 1)
    rounds = [2**i for i in range(nh.bit_length()) if 2 * 2**i < nh]

    waits = []

    def send(device, source, target, which, condition=None):
        copy = pltpu.make_async_remote_copy(
            src_ref=source,
            dst_ref=target,
            send_sem=send_sem.at[len(waits)],
            recv_sem=recv_sem.at[which],
            device_id=device,
            device_id_type=MESH,
        )
        waits.append((copy, condition))
        if condition is None:
            copy.start()
        else:
            pl.when(condition)(copy.start)

    def await_bytes(buffer, which):
        pltpu.make_async_remote_copy(
            src_ref=buffer,
            dst_ref=buffer,
            send_sem=send_sem.at[0],
            recv_sem=recv_sem.at[which],
            device_id={"ctx": ctx_pos + 1 - 2 * core},
            device_id_type=MESH,
        ).wait_recv()

    twin = {"ctx": ctx_pos + 1 - 2 * core}

    loads[6].wait()
    starts = []
    running = jnp.int32(0)
    for r in range(lengths.shape[0]):
        starts.append(running)
        running = running + lengths[r]

    def request_at(position):
        total = jnp.zeros(position.shape, F32)
        for start in starts:
            total = total + jnp.where(position >= start, 1.0, 0.0)
        return total

    chunk_first = ctx_pos * tokens + iota((chunks, CHUNK), 0) * CHUNK
    request = request_at(chunk_first + iota((chunks, CHUNK), 1))
    request_end = request_at(chunk_first + (CHUNK - 1))
    request_prior = request_at(chunk_first - 1)
    live_end = jnp.where(request == request_end, 1.0, 0.0)
    live_start = jnp.where(request == request_prior, 1.0, 0.0)
    requests[...] = request

    row = iota((CHUNK, lanes), 0)
    row = jnp.where(row >= HALF, row - HALF, row)
    head_of_lane = iota((CHUNK, lanes), 1) // width
    for kind in range(KINDS):
        spread[kind] = jnp.where(row == kind * ROWS + head_of_lane, 1.0, 0.0).astype(BF16)
    spread_request[...] = jnp.where(iota((CHUNK, CHUNK), 0) == REQUEST_ROW, 1.0, 0.0).astype(BF16)

    loads[0].wait()
    upper = jnp.where(iota((CHUNK, CHUNK), 0) <= iota((CHUNK, CHUNK), 1), 1.0, 0.0)
    stacked = jnp.concatenate([decay[:, k * CHUNK : (k + 1) * CHUNK] for k in range(chunks)], axis=0)
    cum = jnp.dot(stacked, upper, preferred_element_type=F32, precision=lax.Precision.HIGHEST)
    before = jnp.ones((ROWS, CHUNK), F32)
    for k in range(chunks):
        part = cum[k * ROWS : (k + 1) * ROWS]
        middle = jnp.broadcast_to(part[:, HALF - 1 : HALF], part.shape)
        end = jnp.broadcast_to(part[:, CHUNK - 1 :], part.shape)
        from_start = jnp.exp(part) * live_start[k : k + 1]
        factors = [
            jnp.exp(end - part) * live_end[k : k + 1],
            jnp.exp(middle - part),
            jnp.exp(part - middle),
            from_start,
            from_start * before,
        ]
        before = before * jnp.broadcast_to(from_start[:, CHUNK - 1 :], part.shape)
        values = jnp.concatenate(factors, axis=0)
        high = values.astype(BF16).astype(F32)
        request_rows = jnp.broadcast_to(request[k : k + 1], (ROWS, CHUNK))
        blank = jnp.zeros((HALF - REQUEST_ROW - ROWS, CHUNK), F32)
        blank_low = jnp.zeros((HALF - REQUEST_ROW, CHUNK), F32)
        whole = jnp.concatenate([high, request_rows, blank, values - high, blank_low], axis=0)
        table[k] = whole.T.astype(BF16)
    decay_out[...] = table[chunks - 1, CHUNK - 16 :, :].astype(F32)[15:16]
    leaving[...] = matmul(table[:, CHUNK - 16 :, :].reshape(16 * chunks, CHUNK), spread[FROM_CHUNK])

    loads[1].wait()
    for k in range(chunks):
        b_turned[k] = b[k * CHUNK : (k + 1) * CHUNK, :].T
    loads[2].wait()
    mine = pl.ds(pl.multiple_of(core * share, share), share)
    others = pl.ds(pl.multiple_of((1 - core) * share, share), share)
    for half, part, which in ((1 - core, others, FIRST_HALF), (core, mine, SECOND_HALF)):
        entering = jnp.zeros((state_size, share), F32)
        for k in range(chunks):
            rows = slice(k * CHUNK, (k + 1) * CHUNK)
            local_state[k, :, part] = entering.astype(BF16)
            scaled = (x[rows, part].astype(F32) * matmul(table[k], spread[TO_END, :, part])).astype(BF16)
            entering = leaving[16 * k + 15 : 16 * k + 16, part] * entering + matmul(b_turned[k], scaled)
        state_out[half] = entering
        if which == FIRST_HALF:
            pl.semaphore_wait(barrier, 2 * side + 2)
            if rounds:
                signal_heads(ready.at[0], rounds[0])
            send(twin, decay_out, decay_in, DECAY)
        send(twin, state_out.at[half], state_in.at[half], which, None if which == FIRST_HALF else core == 0)

    await_bytes(decay_in, DECAY)
    both = jnp.concatenate([decay_out[...], decay_in[...]] * (ROWS // 2), axis=0).astype(BF16)
    decays[...] = matmul(both, spread[FROM_DEVICE])
    await_bytes(state_in.at[0], FIRST_HALF)
    first_core = core == 0
    own_state, own_decay = state_out[core], decays[0:1, mine]
    got_state, got_decay = state_in[core], decays[1:2, mine]
    joined = jnp.where(first_core, own_state, got_state) * jnp.where(first_core, got_decay, own_decay)
    joined = joined + jnp.where(first_core, got_state, own_state)
    step_out[...] = own_decay * got_decay
    for i in range(side):
        slice_out[i] = joined[i * share_rows : (i + 1) * share_rows]
    for along in sorted(range(side), key=lambda along: -around(along, side)):
        other = device_at(1, along)
        column = lax.rem(chip_column + along, side)
        send({"ctx": other}, step_out, step_in.at[chip_column], STEP_BEFORE, not_last_row)
        send({"ctx": other}, slice_out.at[column], slice_in.at[chip_column], SLICE_BEFORE, not_last_row)
    for along in sorted(range(1, side), key=lambda along: -around(along, side)):
        other = device_at(0, along)
        column = lax.rem(chip_column + along, side)
        send({"ctx": other}, step_out, step_in.at[side + chip_column], STEP)
        send({"ctx": other}, slice_out.at[column], slice_in.at[side + chip_column], SLICE)
    step_in[side + chip_column] = step_out[...]
    slice_in[side + chip_column] = slice_out[chip_column]

    @pl.when(chip_row == 0)
    def _():
        step_in[0:side] = jnp.zeros((side, 1, share), F32)
        slice_in[0:side] = jnp.zeros((side, share_rows, share), F32)

    loads[3].wait()
    loads[4].wait()
    loads[5].wait()
    lane_head = iota((1, lanes), 1) // width
    skip_row = jnp.zeros((1, lanes), F32)
    for h in range(ROWS):
        skip_row = jnp.where(lane_head == h, skip[h], skip_row)
    causal = iota((CHUNK, CHUNK), 0) >= iota((CHUNK, CHUNK), 1)

    def own_part(k):
        rows = slice(k * CHUNK, (k + 1) * CHUNK)
        maps = c[rows, :]
        same = matmul(table[k], spread_request[...]) == requests[k : k + 1, :]
        scores = jnp.where(causal & same, matmul(maps, b_turned[k]), 0.0).astype(BF16)
        wide = x[rows, :].astype(F32)
        keys = (wide * matmul(table[k], spread[TO_KEY])).astype(BF16)
        total = matmul(scores, keys) * matmul(table[k], spread[TO_QUERY])
        total += matmul(maps, local_state[k]) * matmul(table[k], spread[FROM_CHUNK])
        partial[rows, :] = total + skip_row * wide
        from_device[rows, :] = matmul(table[k], spread[FROM_DEVICE])
        branch = z[rows, :].astype(F32)
        gate[rows, :] = branch / (1.0 + jnp.exp(-branch))

    for k in range(chunks):
        own_part(k)

    def hear(i):
        pl.semaphore_wait(ready.at[i], 2)
        if i + 1 < len(rounds):
            signal_heads(ready.at[i + 1], rounds[i + 1])

    for i in range(len(rounds))[:1]:
        hear(i)

    @pl.when(not_first_row)
    def _():
        await_bytes(step_in.at[0:side], STEP_BEFORE)
        await_bytes(slice_in.at[0:side], SLICE_BEFORE)

    await_bytes(step_in.at[0 : side - 1], STEP)
    await_bytes(slice_in.at[0 : side - 1], SLICE)
    entering = slice_in[0]
    for i in range(1, 2 * side):
        if i >= side:
            enter_out[i - side] = entering
        entering = step_in[i] * entering + slice_in[i] if i < 2 * side - 1 else entering
    for along in sorted(range(1, side), key=lambda along: -around(along, side)):
        column = lax.rem(chip_column + along, side)
        send(
            {"ctx": device_at(0, along)}, enter_out.at[column], enter_in.at[chip_column], ENTER,
            not_first_row | (column > 0),
        )
    for i in range(len(rounds))[1:2]:
        hear(i)

    @pl.when(chip > 0)
    def _():
        enter_in[chip_column] = enter_out[chip_column]
        await_bytes(enter_in.at[0 : side - 1], ENTER)

    send(twin, enter_in, enter_other, SWAP, chip > 0)

    @pl.when(chip > 0)
    def _():
        state[:, mine] = enter_in[...].reshape(state_size, share)
        await_bytes(enter_other, SWAP)
        state[:, others] = enter_other[...].reshape(state_size, share)

    @pl.when(chip == 0)
    def _():
        state[...] = jnp.zeros(state.shape, F32)

    @pl.when(core == 1)
    def _():
        await_bytes(state_in.at[0], SECOND_HALF)
        before_core = jnp.concatenate([state_in[0], state_in[1]], axis=1)
        state[...] = decays[1:2, :] * state[...] + before_core

    entered = state[...].astype(BF16)

    step_rows = 2 * CHUNK
    for k in range(tokens // step_rows):
        rows = slice(k * step_rows, (k + 1) * step_rows)
        output = partial[rows, :] + matmul(c[rows, :], entered) * from_device[rows, :]
        gates = output.astype(BF16).astype(F32) * gate[rows, :]
        gated[rows, :] = gates
        squared = gates * gates
        folded = squared[:, :CHUNK]
        for i in range(1, lanes // CHUNK):
            folded = folded + squared[:, i * CHUNK : (i + 1) * CHUNK]
        for i in range(2):
            square_out[2 * k + i : 2 * k + i + 1, :] = jnp.sum(
                folded[i * CHUNK : (i + 1) * CHUNK].T, axis=0, keepdims=True
            )

    for i in range(len(rounds))[2:]:
        hear(i)
    for offset in sorted(range(1, nh), key=lambda offset: -around(offset, nh)):
        send({"head": lax.rem(head_pos + offset, nh)}, square_out, square_in.at[head_pos], SQUARE)
    square_in[head_pos] = square_out[...]
    await_bytes(square_in.at[0 : nh - 1], SQUARE)
    squares = square_in[0]
    for i in range(1, nh):
        squares = squares + square_in[i]
    scales[...] = lax.rsqrt(squares / (nh * lanes) + EPS)
    for copy, condition in waits:
        if condition is None:
            copy.wait_send()
        else:
            pl.when(condition)(copy.wait_send)


def normalize(gated, scales, gain, out_hbm, out, sem):
    tokens, lanes = gated.shape
    copies = []
    for k in range(tokens // CHUNK):
        rows = slice(k * CHUNK, (k + 1) * CHUNK)
        scale = jnp.broadcast_to(scales[k : k + 1, :], (CHUNK, CHUNK)).T
        scale = jnp.concatenate([scale] * (lanes // CHUNK), axis=1)
        out[rows, :] = (gated[rows, :] * scale * gain[...]).astype(BF16)
        copies.append(pltpu.make_async_copy(out.at[rows, :], out_hbm.at[rows, :], sem.at[k]))
        copies[-1].start()
    for copy in copies:
        copy.wait()


def on_device(nh, nc, head_inputs, gate_z, input_b, output_c, log_decay, lengths, skip_coef, norm_gain):
    tokens, lanes = head_inputs.shape
    heads = skip_coef.shape[0]
    assert heads == ROWS and tokens == ROWS * CHUNK
    state_size = CHUNK
    groups = input_b.shape[1] // state_size
    chunks = tokens // CHUNK
    share = lanes // 2
    side = math.isqrt(nc // 2)
    share_rows = state_size // side
    vmem, smem, hbm = pltpu.VMEM, pltpu.SMEM, pltpu.HBM
    gated, scales = pl.pallas_call(
        functools.partial(kernel, nh, nc, heads * nh // groups),
        out_shape=(
            jax.ShapeDtypeStruct((tokens, lanes), F32),
            jax.ShapeDtypeStruct((chunks, CHUNK), F32),
        ),
        in_specs=[pl.BlockSpec(memory_space=hbm)] * 7,
        out_specs=(pl.BlockSpec(memory_space=vmem), pl.BlockSpec(memory_space=vmem)),
        scratch_shapes=[
            smem(lengths.shape, jnp.int32),
            smem(skip_coef.shape, F32),
            vmem((tokens, lanes), BF16),
            vmem((tokens, lanes), BF16),
            vmem((tokens, state_size), BF16),
            vmem((tokens, state_size), BF16),
            vmem((chunks, state_size, CHUNK), BF16),
            vmem((heads, tokens), F32),
            vmem((chunks, CHUNK, CHUNK), BF16),
            vmem((KINDS, CHUNK, lanes), BF16),
            vmem((CHUNK, CHUNK), BF16),
            vmem((chunks, CHUNK), F32),
            vmem((16 * chunks, lanes), F32),
            vmem((chunks, state_size, lanes), BF16),
            vmem((state_size, lanes), F32),
            vmem((tokens, lanes), F32),
            vmem((tokens, lanes), F32),
            vmem((tokens, lanes), F32),
            vmem((1, CHUNK), F32),
            vmem((1, CHUNK), F32),
            vmem((heads, lanes), F32),
            vmem((2, state_size, share), F32),
            vmem((2, state_size, share), F32),
            vmem((1, share), F32),
            vmem((2 * side, 1, share), F32),
            vmem((side, share_rows, share), F32),
            vmem((2 * side, share_rows, share), F32),
            vmem((side, share_rows, share), F32),
            vmem((side, share_rows, share), F32),
            vmem((side, share_rows, share), F32),
            vmem((chunks, CHUNK), F32),
            vmem((nh, chunks, CHUNK), F32),
            pltpu.SemaphoreType.DMA((7,)),
            pltpu.SemaphoreType.DMA((6 * side + nh + 4,)),
            pltpu.SemaphoreType.DMA((10,)),
            pltpu.SemaphoreType.REGULAR((4,)),
        ],
        compiler_params=pltpu.CompilerParams(
            collective_id=0, has_side_effects=True, vmem_limit_bytes=24 << 20
        ),
    )(*(
        pltpu.with_memory_space_constraint(operand, hbm)
        for operand in (lengths, skip_coef, head_inputs, gate_z, input_b, output_c, log_decay.T)
    ))
    return pl.pallas_call(
        normalize,
        out_shape=jax.ShapeDtypeStruct((tokens, lanes), BF16),
        in_specs=[pl.BlockSpec(memory_space=vmem)] * 3,
        out_specs=pl.BlockSpec(memory_space=hbm),
        scratch_shapes=[vmem((tokens, lanes), BF16), pltpu.SemaphoreType.DMA((chunks,))],
        compiler_params=pltpu.CompilerParams(vmem_limit_bytes=8 << 20),
    )(gated, scales, norm_gain.reshape(1, lanes))


def solution(mesh):
    return jax.shard_map(
        functools.partial(on_device, mesh.shape["head"], mesh.shape["ctx"]),
        mesh=mesh,
        in_specs=(
            P("ctx", "head"),
            P("ctx", "head"),
            P("ctx", None),
            P("ctx", None),
            P("ctx", "head"),
            P(),
            P("head"),
            P("head"),
        ),
        out_specs=P("ctx", "head"),
        check_vma=False,
    )
```

```python
import functools
import math

import jax
import jax.numpy as jnp
from jax import lax
from jax.experimental import pallas as pl
from jax.experimental.pallas import tpu as pltpu
from jax.sharding import PartitionSpec as P

MESH = pl.DeviceIdType.MESH
CHUNK = 128
HALF = CHUNK // 2
ROWS = 8
EPS = 1e-05
TO_END, TO_KEY, TO_QUERY, FROM_CHUNK, FROM_DEVICE = range(5)
KINDS = 5
REQUEST_ROW = KINDS * ROWS
DECAY, FIRST_HALF, SECOND_HALF, BEFORE, STEP, SLICE, ENTER, SWAP, SQUARE = range(9)
F32, BF16 = jnp.float32, jnp.bfloat16


def iota(shape, dim):
    return lax.broadcasted_iota(jnp.int32, shape, dim)


def matmul(left, right):
    return jnp.dot(left, right, preferred_element_type=F32)


def around(offset, count):
    return min(offset, count - offset)


def kernel(
    nh, nc, group_heads, lengths_hbm, skip_hbm, x_hbm, z_hbm, b_hbm, c_hbm, decay_hbm, gated, scales,
    lengths, skip, x, z, b, c, b_turned, decay, table, spread, spread_request, requests, leaving, local_state, state,
    partial, gate, from_device, decay_out, decay_in, decays, state_out, state_in, step_out, step_in,
    slice_out, slice_in, before_out, before_in, enter_out, enter_in, enter_other, square_out, square_in,
    load_sem, send_sem, recv_sem, ready,
):
    head_pos = lax.axis_index("head")
    ctx_pos = lax.axis_index("ctx")
    tokens, lanes = x.shape
    chunks = tokens // CHUNK
    width = lanes // ROWS
    state_size = b.shape[1]
    share_rows, share = slice_in.shape[1:]
    group = head_pos * ROWS // group_heads
    columns = pl.ds(pl.multiple_of(group * state_size, state_size), state_size)
    loads = [
        pltpu.make_async_copy(decay_hbm, decay, load_sem.at[0]),
        pltpu.make_async_copy(b_hbm.at[:, columns], b, load_sem.at[1]),
        pltpu.make_async_copy(x_hbm, x, load_sem.at[2]),
        pltpu.make_async_copy(c_hbm.at[:, columns], c, load_sem.at[3]),
        pltpu.make_async_copy(z_hbm, z, load_sem.at[4]),
        pltpu.make_async_copy(skip_hbm, skip, load_sem.at[5]),
        pltpu.make_async_copy(lengths_hbm, lengths, load_sem.at[6]),
    ]
    for i in (6, 0, 1, 2, 3, 4, 5):
        loads[i].start()

    barrier = pltpu.get_barrier_semaphore()

    side = math.isqrt(nc // 2)
    core = lax.rem(ctx_pos, 2)
    chip = ctx_pos // 2
    chip_row, chip_column = chip // side, lax.rem(chip, side)
    not_first_row, not_last_row = chip_row > 0, chip_row < side - 1

    def device_at(down, along):
        return (lax.rem(chip_row + down, side) * side + lax.rem(chip_column + along, side)) * 2 + core

    def signal_ctx(other):
        pl.semaphore_signal(barrier, inc=1, device_id={"ctx": other}, device_id_type=MESH)

    def signal_heads(semaphore, distance):
        for offset in (distance, nh - distance):
            pl.semaphore_signal(
                semaphore, inc=1, device_id={"head": lax.rem(head_pos + offset, nh)}, device_id_type=MESH
            )

    signal_ctx(ctx_pos + 1 - 2 * core)
    for along in range(1, side):
        signal_ctx(device_at(0, along))
    signal_ctx(device_at(side - 1, 0))
    signal_heads(barrier, 1)
    rounds = [2**i for i in range(nh.bit_length()) if 2 * 2**i < nh]

    waits = []

    def send(device, source, target, which, condition=None):
        copy = pltpu.make_async_remote_copy(
            src_ref=source,
            dst_ref=target,
            send_sem=send_sem.at[len(waits)],
            recv_sem=recv_sem.at[which],
            device_id=device,
            device_id_type=MESH,
        )
        waits.append((copy, condition))
        if condition is None:
            copy.start()
        else:
            pl.when(condition)(copy.start)

    def await_bytes(buffer, which):
        pltpu.make_async_remote_copy(
            src_ref=buffer,
            dst_ref=buffer,
            send_sem=send_sem.at[0],
            recv_sem=recv_sem.at[which],
            device_id={"ctx": ctx_pos + 1 - 2 * core},
            device_id_type=MESH,
        ).wait_recv()

    twin = {"ctx": ctx_pos + 1 - 2 * core}

    loads[6].wait()
    starts = []
    running = jnp.int32(0)
    for r in range(lengths.shape[0]):
        starts.append(running)
        running = running + lengths[r]

    def request_at(position):
        total = jnp.zeros(position.shape, F32)
        for start in starts:
            total = total + jnp.where(position >= start, 1.0, 0.0)
        return total

    chunk_first = ctx_pos * tokens + iota((chunks, CHUNK), 0) * CHUNK
    request = request_at(chunk_first + iota((chunks, CHUNK), 1))
    request_end = request_at(chunk_first + (CHUNK - 1))
    request_prior = request_at(chunk_first - 1)
    live_end = jnp.where(request == request_end, 1.0, 0.0)
    live_start = jnp.where(request == request_prior, 1.0, 0.0)
    requests[...] = request

    row = iota((CHUNK, lanes), 0)
    row = jnp.where(row >= HALF, row - HALF, row)
    head_of_lane = iota((CHUNK, lanes), 1) // width
    for kind in range(KINDS):
        spread[kind] = jnp.where(row == kind * ROWS + head_of_lane, 1.0, 0.0).astype(BF16)
    spread_request[...] = jnp.where(iota((CHUNK, CHUNK), 0) == REQUEST_ROW, 1.0, 0.0).astype(BF16)

    loads[0].wait()
    upper = jnp.where(iota((CHUNK, CHUNK), 0) <= iota((CHUNK, CHUNK), 1), 1.0, 0.0)
    stacked = jnp.concatenate([decay[:, k * CHUNK : (k + 1) * CHUNK] for k in range(chunks)], axis=0)
    cum = jnp.dot(stacked, upper, preferred_element_type=F32, precision=lax.Precision.HIGHEST)
    before = jnp.ones((ROWS, CHUNK), F32)
    for k in range(chunks):
        part = cum[k * ROWS : (k + 1) * ROWS]
        middle = jnp.broadcast_to(part[:, HALF - 1 : HALF], part.shape)
        end = jnp.broadcast_to(part[:, CHUNK - 1 :], part.shape)
        from_start = jnp.exp(part) * live_start[k : k + 1]
        factors = [
            jnp.exp(end - part) * live_end[k : k + 1],
            jnp.exp(middle - part),
            jnp.exp(part - middle),
            from_start,
            from_start * before,
        ]
        before = before * jnp.broadcast_to(from_start[:, CHUNK - 1 :], part.shape)
        values = jnp.concatenate(factors, axis=0)
        high = values.astype(BF16).astype(F32)
        request_rows = jnp.broadcast_to(request[k : k + 1], (ROWS, CHUNK))
        blank = jnp.zeros((HALF - REQUEST_ROW - ROWS, CHUNK), F32)
        blank_low = jnp.zeros((HALF - REQUEST_ROW, CHUNK), F32)
        whole = jnp.concatenate([high, request_rows, blank, values - high, blank_low], axis=0)
        table[k] = whole.T.astype(BF16)
    decay_out[...] = table[chunks - 1, CHUNK - 16 :, :].astype(F32)[15:16]
    leaving[...] = matmul(table[:, CHUNK - 16 :, :].reshape(16 * chunks, CHUNK), spread[FROM_CHUNK])

    loads[1].wait()
    for k in range(chunks):
        b_turned[k] = b[k * CHUNK : (k + 1) * CHUNK, :].T
    loads[2].wait()
    mine = pl.ds(pl.multiple_of(core * share, share), share)
    others = pl.ds(pl.multiple_of((1 - core) * share, share), share)
    for half, part, which in ((1 - core, others, FIRST_HALF), (core, mine, SECOND_HALF)):
        entering = jnp.zeros((state_size, share), F32)
        for k in range(chunks):
            rows = slice(k * CHUNK, (k + 1) * CHUNK)
            local_state[k, :, part] = entering.astype(BF16)
            scaled = (x[rows, part].astype(F32) * matmul(table[k], spread[TO_END, :, part])).astype(BF16)
            entering = leaving[16 * k + 15 : 16 * k + 16, part] * entering + matmul(b_turned[k], scaled)
        state_out[half] = entering
        if which == FIRST_HALF:
            pl.semaphore_wait(barrier, side + 3)
            if rounds:
                signal_heads(ready.at[0], rounds[0])
            send(twin, decay_out, decay_in, DECAY)
        send(twin, state_out.at[half], state_in.at[half], which, None if which == FIRST_HALF else core == 0)

    await_bytes(decay_in, DECAY)
    both = jnp.concatenate([decay_out[...], decay_in[...]] * (ROWS // 2), axis=0).astype(BF16)
    decays[...] = matmul(both, spread[FROM_DEVICE])
    await_bytes(state_in.at[0], FIRST_HALF)
    first_core = core == 0
    own_state, own_decay = state_out[core], decays[0:1, mine]
    got_state, got_decay = state_in[core], decays[1:2, mine]
    joined = jnp.where(first_core, own_state, got_state) * jnp.where(first_core, got_decay, own_decay)
    joined = joined + jnp.where(first_core, got_state, own_state)
    step_out[...] = own_decay * got_decay
    for i in range(side):
        slice_out[i] = joined[i * share_rows : (i + 1) * share_rows]
    for along in sorted(range(1, side), key=lambda along: -around(along, side)):
        other = device_at(0, along)
        column = lax.rem(chip_column + along, side)
        send({"ctx": other}, step_out, step_in.at[chip_column], STEP)
        send({"ctx": other}, slice_out.at[column], slice_in.at[chip_column], SLICE)
    step_in[chip_column] = step_out[...]
    slice_in[chip_column] = slice_out[chip_column]

    loads[3].wait()
    loads[4].wait()
    loads[5].wait()
    lane_head = iota((1, lanes), 1) // width
    skip_row = jnp.zeros((1, lanes), F32)
    for h in range(ROWS):
        skip_row = jnp.where(lane_head == h, skip[h], skip_row)
    causal = iota((CHUNK, CHUNK), 0) >= iota((CHUNK, CHUNK), 1)

    def own_part(k):
        rows = slice(k * CHUNK, (k + 1) * CHUNK)
        maps = c[rows, :]
        same = matmul(table[k], spread_request[...]) == requests[k : k + 1, :]
        scores = jnp.where(causal & same, matmul(maps, b_turned[k]), 0.0).astype(BF16)
        wide = x[rows, :].astype(F32)
        keys = (wide * matmul(table[k], spread[TO_KEY])).astype(BF16)
        total = matmul(scores, keys) * matmul(table[k], spread[TO_QUERY])
        total += matmul(maps, local_state[k]) * matmul(table[k], spread[FROM_CHUNK])
        partial[rows, :] = total + skip_row * wide
        from_device[rows, :] = matmul(table[k], spread[FROM_DEVICE])
        branch = z[rows, :].astype(F32)
        gate[rows, :] = branch / (1.0 + jnp.exp(-branch))

    for k in range(chunks):
        own_part(k)

    def hear(i):
        pl.semaphore_wait(ready.at[i], 2)
        if i + 1 < len(rounds):
            signal_heads(ready.at[i + 1], rounds[i + 1])

    for i in range(len(rounds))[:1]:
        hear(i)

    await_bytes(step_in.at[0 : side - 1], STEP)
    await_bytes(slice_in.at[0 : side - 1], SLICE)
    leaving_row = slice_in[0]
    for i in range(1, side):
        leaving_row = step_in[i] * leaving_row + slice_in[i]
    before_out[...] = leaving_row
    send({"ctx": device_at(1, 0)}, before_out, before_in, BEFORE, not_last_row)

    @pl.when(not_first_row)
    def _():
        await_bytes(before_in, BEFORE)

    @pl.when(chip_row == 0)
    def _():
        before_in[...] = jnp.zeros(before_in.shape, F32)

    entering = before_in[...]
    for i in range(side):
        enter_out[i] = entering
        if i < side - 1:
            entering = step_in[i] * entering + slice_in[i]
    for along in sorted(range(1, side), key=lambda along: -around(along, side)):
        column = lax.rem(chip_column + along, side)
        send(
            {"ctx": device_at(0, along)}, enter_out.at[column], enter_in.at[chip_column], ENTER,
            not_first_row | (column > 0),
        )
    for i in range(len(rounds))[1:2]:
        hear(i)

    @pl.when(chip > 0)
    def _():
        enter_in[chip_column] = enter_out[chip_column]
        await_bytes(enter_in.at[0 : side - 1], ENTER)

    send(twin, enter_in, enter_other, SWAP, chip > 0)

    @pl.when(chip > 0)
    def _():
        state[:, mine] = enter_in[...].reshape(state_size, share)
        await_bytes(enter_other, SWAP)
        state[:, others] = enter_other[...].reshape(state_size, share)

    @pl.when(chip == 0)
    def _():
        state[...] = jnp.zeros(state.shape, F32)

    @pl.when(core == 1)
    def _():
        await_bytes(state_in.at[0], SECOND_HALF)
        before_core = jnp.concatenate([state_in[0], state_in[1]], axis=1)
        state[...] = decays[1:2, :] * state[...] + before_core

    entered = state[...].astype(BF16)

    step_rows = 2 * CHUNK
    for k in range(tokens // step_rows):
        rows = slice(k * step_rows, (k + 1) * step_rows)
        output = partial[rows, :] + matmul(c[rows, :], entered) * from_device[rows, :]
        gates = output.astype(BF16).astype(F32) * gate[rows, :]
        gated[rows, :] = gates
        squared = gates * gates
        folded = squared[:, :CHUNK]
        for i in range(1, lanes // CHUNK):
            folded = folded + squared[:, i * CHUNK : (i + 1) * CHUNK]
        for i in range(2):
            square_out[2 * k + i : 2 * k + i + 1, :] = jnp.sum(
                folded[i * CHUNK : (i + 1) * CHUNK].T, axis=0, keepdims=True
            )

    for i in range(len(rounds))[2:]:
        hear(i)
    for offset in sorted(range(1, nh), key=lambda offset: -around(offset, nh)):
        send({"head": lax.rem(head_pos + offset, nh)}, square_out, square_in.at[head_pos], SQUARE)
    square_in[head_pos] = square_out[...]
    await_bytes(square_in.at[0 : nh - 1], SQUARE)
    squares = square_in[0]
    for i in range(1, nh):
        squares = squares + square_in[i]
    scales[...] = lax.rsqrt(squares / (nh * lanes) + EPS)
    for copy, condition in waits:
        if condition is None:
            copy.wait_send()
        else:
            pl.when(condition)(copy.wait_send)


def normalize(gated, scales, gain, out_hbm, out, sem):
    tokens, lanes = gated.shape
    copies = []
    for k in range(tokens // CHUNK):
        rows = slice(k * CHUNK, (k + 1) * CHUNK)
        scale = jnp.broadcast_to(scales[k : k + 1, :], (CHUNK, CHUNK)).T
        scale = jnp.concatenate([scale] * (lanes // CHUNK), axis=1)
        out[rows, :] = (gated[rows, :] * scale * gain[...]).astype(BF16)
        copies.append(pltpu.make_async_copy(out.at[rows, :], out_hbm.at[rows, :], sem.at[k]))
        copies[-1].start()
    for copy in copies:
        copy.wait()


def on_device(nh, nc, head_inputs, gate_z, input_b, output_c, log_decay, lengths, skip_coef, norm_gain):
    tokens, lanes = head_inputs.shape
    heads = skip_coef.shape[0]
    assert heads == ROWS and tokens == ROWS * CHUNK
    state_size = CHUNK
    groups = input_b.shape[1] // state_size
    chunks = tokens // CHUNK
    share = lanes // 2
    side = math.isqrt(nc // 2)
    share_rows = state_size // side
    vmem, smem, hbm = pltpu.VMEM, pltpu.SMEM, pltpu.HBM
    gated, scales = pl.pallas_call(
        functools.partial(kernel, nh, nc, heads * nh // groups),
        out_shape=(
            jax.ShapeDtypeStruct((tokens, lanes), F32),
            jax.ShapeDtypeStruct((chunks, CHUNK), F32),
        ),
        in_specs=[pl.BlockSpec(memory_space=hbm)] * 7,
        out_specs=(pl.BlockSpec(memory_space=vmem), pl.BlockSpec(memory_space=vmem)),
        scratch_shapes=[
            smem(lengths.shape, jnp.int32),
            smem(skip_coef.shape, F32),
            vmem((tokens, lanes), BF16),
            vmem((tokens, lanes), BF16),
            vmem((tokens, state_size), BF16),
            vmem((tokens, state_size), BF16),
            vmem((chunks, state_size, CHUNK), BF16),
            vmem((heads, tokens), F32),
            vmem((chunks, CHUNK, CHUNK), BF16),
            vmem((KINDS, CHUNK, lanes), BF16),
            vmem((CHUNK, CHUNK), BF16),
            vmem((chunks, CHUNK), F32),
            vmem((16 * chunks, lanes), F32),
            vmem((chunks, state_size, lanes), BF16),
            vmem((state_size, lanes), F32),
            vmem((tokens, lanes), F32),
            vmem((tokens, lanes), F32),
            vmem((tokens, lanes), F32),
            vmem((1, CHUNK), F32),
            vmem((1, CHUNK), F32),
            vmem((heads, lanes), F32),
            vmem((2, state_size, share), F32),
            vmem((2, state_size, share), F32),
            vmem((1, share), F32),
            vmem((side, 1, share), F32),
            vmem((side, share_rows, share), F32),
            vmem((side, share_rows, share), F32),
            vmem((share_rows, share), F32),
            vmem((share_rows, share), F32),
            vmem((side, share_rows, share), F32),
            vmem((side, share_rows, share), F32),
            vmem((side, share_rows, share), F32),
            vmem((chunks, CHUNK), F32),
            vmem((nh, chunks, CHUNK), F32),
            pltpu.SemaphoreType.DMA((7,)),
            pltpu.SemaphoreType.DMA((6 * side + nh + 4,)),
            pltpu.SemaphoreType.DMA((10,)),
            pltpu.SemaphoreType.REGULAR((4,)),
        ],
        compiler_params=pltpu.CompilerParams(
            collective_id=0, has_side_effects=True, vmem_limit_bytes=24 << 20
        ),
    )(*(
        pltpu.with_memory_space_constraint(operand, hbm)
        for operand in (lengths, skip_coef, head_inputs, gate_z, input_b, output_c, log_decay.T)
    ))
    return pl.pallas_call(
        normalize,
        out_shape=jax.ShapeDtypeStruct((tokens, lanes), BF16),
        in_specs=[pl.BlockSpec(memory_space=vmem)] * 3,
        out_specs=pl.BlockSpec(memory_space=hbm),
        scratch_shapes=[vmem((tokens, lanes), BF16), pltpu.SemaphoreType.DMA((chunks,))],
        compiler_params=pltpu.CompilerParams(vmem_limit_bytes=8 << 20),
    )(gated, scales, norm_gain.reshape(1, lanes))


def solution(mesh):
    return jax.shard_map(
        functools.partial(on_device, mesh.shape["head"], mesh.shape["ctx"]),
        mesh=mesh,
        in_specs=(
            P("ctx", "head"),
            P("ctx", "head"),
            P("ctx", None),
            P("ctx", None),
            P("ctx", "head"),
            P(),
            P("head"),
            P("head"),
        ),
        out_specs=P("ctx", "head"),
        check_vma=False,
    )
```

```python
import functools
import math

import jax
import jax.numpy as jnp
from jax import lax
from jax.experimental import pallas as pl
from jax.experimental.pallas import tpu as pltpu
from jax.sharding import PartitionSpec as P

MESH = pl.DeviceIdType.MESH
CHUNK = 128
HALF = CHUNK // 2
ROWS = 8
EPS = 1e-05
TO_END, TO_KEY, TO_QUERY, FROM_CHUNK, FROM_DEVICE = range(5)
KINDS = 5
LATER = 3
REQUEST_ROW = KINDS * ROWS
DECAY, FIRST_HALF, SECOND_HALF, BEFORE, STEP, SLICE, ENTER, SWAP, SQUARE = range(9)
F32, BF16 = jnp.float32, jnp.bfloat16


def iota(shape, dim):
    return lax.broadcasted_iota(jnp.int32, shape, dim)


def matmul(left, right):
    return jnp.dot(left, right, preferred_element_type=F32)


def around(offset, count):
    return min(offset, count - offset)


def kernel(
    nh, nc, group_heads, lengths_hbm, skip_hbm, x_hbm, z_hbm, b_hbm, c_hbm, decay_hbm, gated, scales,
    lengths, skip, x, z, b, c, b_turned, decay, table, spread, spread_request, requests, leaving, local_state, state,
    partial, gate, from_device, decay_out, decay_in, decays, state_out, state_in, step_out, step_in,
    slice_out, slice_in, before_out, before_in, enter_out, enter_in, enter_other, square_out, square_in,
    load_sem, send_sem, recv_sem, ready,
):
    head_pos = lax.axis_index("head")
    ctx_pos = lax.axis_index("ctx")
    tokens, lanes = x.shape
    chunks = tokens // CHUNK
    width = lanes // ROWS
    state_size = b.shape[1]
    share_rows, share = slice_in.shape[1:]
    group = head_pos * ROWS // group_heads
    columns = pl.ds(pl.multiple_of(group * state_size, state_size), state_size)
    loads = [
        pltpu.make_async_copy(decay_hbm, decay, load_sem.at[0]),
        pltpu.make_async_copy(b_hbm.at[:, columns], b, load_sem.at[1]),
        pltpu.make_async_copy(x_hbm, x, load_sem.at[2]),
        pltpu.make_async_copy(c_hbm.at[:, columns], c, load_sem.at[3]),
        pltpu.make_async_copy(z_hbm, z, load_sem.at[4]),
        pltpu.make_async_copy(skip_hbm, skip, load_sem.at[5]),
        pltpu.make_async_copy(lengths_hbm, lengths, load_sem.at[6]),
    ]
    for i in (6, 0, 1, 2, 3, 4, 5):
        loads[i].start()

    barrier = pltpu.get_barrier_semaphore()

    side = math.isqrt(nc // 2)
    core = lax.rem(ctx_pos, 2)
    chip = ctx_pos // 2
    chip_row, chip_column = chip // side, lax.rem(chip, side)
    not_first_row, not_last_row = chip_row > 0, chip_row < side - 1

    def device_at(down, along):
        return (lax.rem(chip_row + down, side) * side + lax.rem(chip_column + along, side)) * 2 + core

    def signal_ctx(other):
        pl.semaphore_signal(barrier, inc=1, device_id={"ctx": other}, device_id_type=MESH)

    def signal_heads(semaphore, distance):
        for offset in (distance, nh - distance):
            pl.semaphore_signal(
                semaphore, inc=1, device_id={"head": lax.rem(head_pos + offset, nh)}, device_id_type=MESH
            )

    signal_ctx(ctx_pos + 1 - 2 * core)
    for along in range(1, side):
        signal_ctx(device_at(0, along))
    signal_ctx(device_at(side - 1, 0))
    signal_heads(barrier, 1)
    rounds = [2**i for i in range(nh.bit_length()) if 2 * 2**i < nh]

    waits = []

    def send(device, source, target, which, condition=None):
        copy = pltpu.make_async_remote_copy(
            src_ref=source,
            dst_ref=target,
            send_sem=send_sem.at[len(waits)],
            recv_sem=recv_sem.at[which],
            device_id=device,
            device_id_type=MESH,
        )
        waits.append((copy, condition))
        if condition is None:
            copy.start()
        else:
            pl.when(condition)(copy.start)

    def await_bytes(buffer, which):
        pltpu.make_async_remote_copy(
            src_ref=buffer,
            dst_ref=buffer,
            send_sem=send_sem.at[0],
            recv_sem=recv_sem.at[which],
            device_id={"ctx": ctx_pos + 1 - 2 * core},
            device_id_type=MESH,
        ).wait_recv()

    twin = {"ctx": ctx_pos + 1 - 2 * core}

    loads[6].wait()
    starts = []
    running = jnp.int32(0)
    for r in range(lengths.shape[0]):
        starts.append(running)
        running = running + lengths[r]

    def request_at(position):
        total = jnp.zeros(position.shape, F32)
        for start in starts:
            total = total + jnp.where(position >= start, 1.0, 0.0)
        return total

    chunk_first = ctx_pos * tokens + iota((chunks, CHUNK), 0) * CHUNK
    request = request_at(chunk_first + iota((chunks, CHUNK), 1))
    request_end = request_at(chunk_first + (CHUNK - 1))
    request_prior = request_at(chunk_first - 1)
    live_end = jnp.where(request == request_end, 1.0, 0.0)
    live_start = jnp.where(request == request_prior, 1.0, 0.0)
    requests[...] = request

    row = iota((CHUNK, lanes), 0)
    row = jnp.where(row >= HALF, row - HALF, row)
    head_of_lane = iota((CHUNK, lanes), 1) // width
    for kind in range(KINDS):
        spread[kind] = jnp.where(row == kind * ROWS + head_of_lane, 1.0, 0.0).astype(BF16)
    spread_request[...] = jnp.where(iota((CHUNK, CHUNK), 0) == REQUEST_ROW, 1.0, 0.0).astype(BF16)

    loads[0].wait()
    upper = jnp.where(iota((CHUNK, CHUNK), 0) <= iota((CHUNK, CHUNK), 1), 1.0, 0.0)
    stacked = jnp.concatenate([decay[:, k * CHUNK : (k + 1) * CHUNK] for k in range(chunks)], axis=0)
    cum = jnp.dot(stacked, upper, preferred_element_type=F32, precision=lax.Precision.HIGHEST)
    before = jnp.ones((ROWS, CHUNK), F32)
    for k in range(chunks):
        part = cum[k * ROWS : (k + 1) * ROWS]
        middle = jnp.broadcast_to(part[:, HALF - 1 : HALF], part.shape)
        end = jnp.broadcast_to(part[:, CHUNK - 1 :], part.shape)
        from_start = jnp.exp(part) * live_start[k : k + 1]
        factors = [
            jnp.exp(end - part) * live_end[k : k + 1],
            jnp.exp(middle - part),
            jnp.exp(part - middle),
            from_start,
            from_start * before,
        ]
        before = before * jnp.broadcast_to(from_start[:, CHUNK - 1 :], part.shape)
        values = jnp.concatenate(factors, axis=0)
        high = values.astype(BF16).astype(F32)
        request_rows = jnp.broadcast_to(request[k : k + 1], (ROWS, CHUNK))
        blank = jnp.zeros((HALF - REQUEST_ROW - ROWS, CHUNK), F32)
        blank_low = jnp.zeros((HALF - REQUEST_ROW, CHUNK), F32)
        whole = jnp.concatenate([high, request_rows, blank, values - high, blank_low], axis=0)
        table[k] = whole.T.astype(BF16)
    decay_out[...] = table[chunks - 1, CHUNK - 16 :, :].astype(F32)[15:16]
    leaving[...] = matmul(table[:, CHUNK - 16 :, :].reshape(16 * chunks, CHUNK), spread[FROM_CHUNK])

    loads[1].wait()
    for k in range(chunks):
        b_turned[k] = b[k * CHUNK : (k + 1) * CHUNK, :].T
    loads[2].wait()
    mine = pl.ds(pl.multiple_of(core * share, share), share)
    others = pl.ds(pl.multiple_of((1 - core) * share, share), share)
    for half, part, which in ((1 - core, others, FIRST_HALF), (core, mine, SECOND_HALF)):
        entering = jnp.zeros((state_size, share), F32)
        for k in range(chunks):
            rows = slice(k * CHUNK, (k + 1) * CHUNK)
            local_state[k, :, part] = entering.astype(BF16)
            scaled = (x[rows, part].astype(F32) * matmul(table[k], spread[TO_END, :, part])).astype(BF16)
            entering = leaving[16 * k + 15 : 16 * k + 16, part] * entering + matmul(b_turned[k], scaled)
        state_out[half] = entering
        if which == FIRST_HALF:
            pl.semaphore_wait(barrier, side + 3)
            if rounds:
                signal_heads(ready.at[0], rounds[0])
            send(twin, decay_out, decay_in, DECAY)
        send(twin, state_out.at[half], state_in.at[half], which, None if which == FIRST_HALF else core == 0)

    await_bytes(decay_in, DECAY)
    both = jnp.concatenate([decay_out[...], decay_in[...]] * (ROWS // 2), axis=0).astype(BF16)
    decays[...] = matmul(both, spread[FROM_DEVICE])
    await_bytes(state_in.at[0], FIRST_HALF)
    first_core = core == 0
    own_state, own_decay = state_out[core], decays[0:1, mine]
    got_state, got_decay = state_in[core], decays[1:2, mine]
    joined = jnp.where(first_core, own_state, got_state) * jnp.where(first_core, got_decay, own_decay)
    joined = joined + jnp.where(first_core, got_state, own_state)
    step_out[...] = own_decay * got_decay
    for i in range(side):
        slice_out[i] = joined[i * share_rows : (i + 1) * share_rows]
    for along in sorted(range(1, side), key=lambda along: -around(along, side)):
        other = device_at(0, along)
        column = lax.rem(chip_column + along, side)
        send({"ctx": other}, step_out, step_in.at[chip_column], STEP)
        send({"ctx": other}, slice_out.at[column], slice_in.at[chip_column], SLICE)
    step_in[chip_column] = step_out[...]
    slice_in[chip_column] = slice_out[chip_column]

    loads[3].wait()
    loads[4].wait()
    loads[5].wait()
    lane_head = iota((1, lanes), 1) // width
    skip_row = jnp.zeros((1, lanes), F32)
    for h in range(ROWS):
        skip_row = jnp.where(lane_head == h, skip[h], skip_row)
    causal = iota((CHUNK, CHUNK), 0) >= iota((CHUNK, CHUNK), 1)

    def own_part(k):
        rows = slice(k * CHUNK, (k + 1) * CHUNK)
        maps = c[rows, :]
        same = matmul(table[k], spread_request[...]) == requests[k : k + 1, :]
        scores = jnp.where(causal & same, matmul(maps, b_turned[k]), 0.0).astype(BF16)
        wide = x[rows, :].astype(F32)
        keys = (wide * matmul(table[k], spread[TO_KEY])).astype(BF16)
        total = matmul(scores, keys) * matmul(table[k], spread[TO_QUERY])
        total += matmul(maps, local_state[k]) * matmul(table[k], spread[FROM_CHUNK])
        partial[rows, :] = total + skip_row * wide
        from_device[rows, :] = matmul(table[k], spread[FROM_DEVICE])
        branch = z[rows, :].astype(F32)
        gate[rows, :] = branch / (1.0 + jnp.exp(-branch))

    for k in range(chunks - LATER):
        own_part(k)

    def hear(i):
        pl.semaphore_wait(ready.at[i], 2)
        if i + 1 < len(rounds):
            signal_heads(ready.at[i + 1], rounds[i + 1])

    await_bytes(step_in.at[0 : side - 1], STEP)
    await_bytes(slice_in.at[0 : side - 1], SLICE)
    leaving_row = slice_in[0]
    for i in range(1, side):
        leaving_row = step_in[i] * leaving_row + slice_in[i]
    before_out[...] = leaving_row
    send({"ctx": device_at(1, 0)}, before_out, before_in, BEFORE, not_last_row)
    for k in range(chunks - LATER, chunks):
        own_part(k)
    for i in range(len(rounds))[:1]:
        hear(i)

    @pl.when(not_first_row)
    def _():
        await_bytes(before_in, BEFORE)

    @pl.when(chip_row == 0)
    def _():
        before_in[...] = jnp.zeros(before_in.shape, F32)

    entering = before_in[...]
    for i in range(side):
        enter_out[i] = entering
        if i < side - 1:
            entering = step_in[i] * entering + slice_in[i]
    for along in sorted(range(1, side), key=lambda along: -around(along, side)):
        column = lax.rem(chip_column + along, side)
        send(
            {"ctx": device_at(0, along)}, enter_out.at[column], enter_in.at[chip_column], ENTER,
            not_first_row | (column > 0),
        )
    for i in range(len(rounds))[1:2]:
        hear(i)

    @pl.when(chip > 0)
    def _():
        enter_in[chip_column] = enter_out[chip_column]
        await_bytes(enter_in.at[0 : side - 1], ENTER)

    send(twin, enter_in, enter_other, SWAP, chip > 0)

    @pl.when(chip > 0)
    def _():
        state[:, mine] = enter_in[...].reshape(state_size, share)
        await_bytes(enter_other, SWAP)
        state[:, others] = enter_other[...].reshape(state_size, share)

    @pl.when(chip == 0)
    def _():
        state[...] = jnp.zeros(state.shape, F32)

    @pl.when(core == 1)
    def _():
        await_bytes(state_in.at[0], SECOND_HALF)
        before_core = jnp.concatenate([state_in[0], state_in[1]], axis=1)
        state[...] = decays[1:2, :] * state[...] + before_core

    entered = state[...].astype(BF16)

    step_rows = 2 * CHUNK
    for k in range(tokens // step_rows):
        rows = slice(k * step_rows, (k + 1) * step_rows)
        output = partial[rows, :] + matmul(c[rows, :], entered) * from_device[rows, :]
        gates = output.astype(BF16).astype(F32) * gate[rows, :]
        gated[rows, :] = gates
        squared = gates * gates
        folded = squared[:, :CHUNK]
        for i in range(1, lanes // CHUNK):
            folded = folded + squared[:, i * CHUNK : (i + 1) * CHUNK]
        for i in range(2):
            square_out[2 * k + i : 2 * k + i + 1, :] = jnp.sum(
                folded[i * CHUNK : (i + 1) * CHUNK].T, axis=0, keepdims=True
            )

    for i in range(len(rounds))[2:]:
        hear(i)
    for offset in sorted(range(1, nh), key=lambda offset: -around(offset, nh)):
        send({"head": lax.rem(head_pos + offset, nh)}, square_out, square_in.at[head_pos], SQUARE)
    square_in[head_pos] = square_out[...]
    await_bytes(square_in.at[0 : nh - 1], SQUARE)
    squares = square_in[0]
    for i in range(1, nh):
        squares = squares + square_in[i]
    scales[...] = lax.rsqrt(squares / (nh * lanes) + EPS)
    for copy, condition in waits:
        if condition is None:
            copy.wait_send()
        else:
            pl.when(condition)(copy.wait_send)


def normalize(gated, scales, gain, out_hbm, out, sem):
    tokens, lanes = gated.shape
    copies = []
    for k in range(tokens // CHUNK):
        rows = slice(k * CHUNK, (k + 1) * CHUNK)
        scale = jnp.broadcast_to(scales[k : k + 1, :], (CHUNK, CHUNK)).T
        scale = jnp.concatenate([scale] * (lanes // CHUNK), axis=1)
        out[rows, :] = (gated[rows, :] * scale * gain[...]).astype(BF16)
        copies.append(pltpu.make_async_copy(out.at[rows, :], out_hbm.at[rows, :], sem.at[k]))
        copies[-1].start()
    for copy in copies:
        copy.wait()


def on_device(nh, nc, head_inputs, gate_z, input_b, output_c, log_decay, lengths, skip_coef, norm_gain):
    tokens, lanes = head_inputs.shape
    heads = skip_coef.shape[0]
    assert heads == ROWS and tokens == ROWS * CHUNK
    state_size = CHUNK
    groups = input_b.shape[1] // state_size
    chunks = tokens // CHUNK
    share = lanes // 2
    side = math.isqrt(nc // 2)
    share_rows = state_size // side
    vmem, smem, hbm = pltpu.VMEM, pltpu.SMEM, pltpu.HBM
    gated, scales = pl.pallas_call(
        functools.partial(kernel, nh, nc, heads * nh // groups),
        out_shape=(
            jax.ShapeDtypeStruct((tokens, lanes), F32),
            jax.ShapeDtypeStruct((chunks, CHUNK), F32),
        ),
        in_specs=[pl.BlockSpec(memory_space=hbm)] * 7,
        out_specs=(pl.BlockSpec(memory_space=vmem), pl.BlockSpec(memory_space=vmem)),
        scratch_shapes=[
            smem(lengths.shape, jnp.int32),
            smem(skip_coef.shape, F32),
            vmem((tokens, lanes), BF16),
            vmem((tokens, lanes), BF16),
            vmem((tokens, state_size), BF16),
            vmem((tokens, state_size), BF16),
            vmem((chunks, state_size, CHUNK), BF16),
            vmem((heads, tokens), F32),
            vmem((chunks, CHUNK, CHUNK), BF16),
            vmem((KINDS, CHUNK, lanes), BF16),
            vmem((CHUNK, CHUNK), BF16),
            vmem((chunks, CHUNK), F32),
            vmem((16 * chunks, lanes), F32),
            vmem((chunks, state_size, lanes), BF16),
            vmem((state_size, lanes), F32),
            vmem((tokens, lanes), F32),
            vmem((tokens, lanes), F32),
            vmem((tokens, lanes), F32),
            vmem((1, CHUNK), F32),
            vmem((1, CHUNK), F32),
            vmem((heads, lanes), F32),
            vmem((2, state_size, share), F32),
            vmem((2, state_size, share), F32),
            vmem((1, share), F32),
            vmem((side, 1, share), F32),
            vmem((side, share_rows, share), F32),
            vmem((side, share_rows, share), F32),
            vmem((share_rows, share), F32),
            vmem((share_rows, share), F32),
            vmem((side, share_rows, share), F32),
            vmem((side, share_rows, share), F32),
            vmem((side, share_rows, share), F32),
            vmem((chunks, CHUNK), F32),
            vmem((nh, chunks, CHUNK), F32),
            pltpu.SemaphoreType.DMA((7,)),
            pltpu.SemaphoreType.DMA((6 * side + nh + 4,)),
            pltpu.SemaphoreType.DMA((10,)),
            pltpu.SemaphoreType.REGULAR((4,)),
        ],
        compiler_params=pltpu.CompilerParams(
            collective_id=0, has_side_effects=True, vmem_limit_bytes=24 << 20
        ),
    )(*(
        pltpu.with_memory_space_constraint(operand, hbm)
        for operand in (lengths, skip_coef, head_inputs, gate_z, input_b, output_c, log_decay.T)
    ))
    return pl.pallas_call(
        normalize,
        out_shape=jax.ShapeDtypeStruct((tokens, lanes), BF16),
        in_specs=[pl.BlockSpec(memory_space=vmem)] * 3,
        out_specs=pl.BlockSpec(memory_space=hbm),
        scratch_shapes=[vmem((tokens, lanes), BF16), pltpu.SemaphoreType.DMA((chunks,))],
        compiler_params=pltpu.CompilerParams(vmem_limit_bytes=8 << 20),
    )(gated, scales, norm_gain.reshape(1, lanes))


def solution(mesh):
    return jax.shard_map(
        functools.partial(on_device, mesh.shape["head"], mesh.shape["ctx"]),
        mesh=mesh,
        in_specs=(
            P("ctx", "head"),
            P("ctx", "head"),
            P("ctx", None),
            P("ctx", None),
            P("ctx", "head"),
            P(),
            P("head"),
            P("head"),
        ),
        out_specs=P("ctx", "head"),
        check_vma=False,
    )
```

```python
import functools
import math

import jax
import jax.numpy as jnp
from jax import lax
from jax.experimental import pallas as pl
from jax.experimental.pallas import tpu as pltpu
from jax.sharding import PartitionSpec as P

MESH = pl.DeviceIdType.MESH
CHUNK = 128
HALF = CHUNK // 2
ROWS = 8
EPS = 1e-05
TO_END, TO_KEY, TO_QUERY, FROM_CHUNK, FROM_DEVICE = range(5)
KINDS = 5
REQUEST_ROW = KINDS * ROWS
DECAY, FIRST_HALF, SECOND_HALF, BEFORE, STEP, SLICE, ENTER, SQUARE = range(8)
F32, BF16 = jnp.float32, jnp.bfloat16


def iota(shape, dim):
    return lax.broadcasted_iota(jnp.int32, shape, dim)


def matmul(left, right):
    return jnp.dot(left, right, preferred_element_type=F32)


def around(offset, count):
    return min(offset, count - offset)


def kernel(
    nh, nc, group_heads, lengths_hbm, skip_hbm, x_hbm, z_hbm, b_hbm, c_hbm, decay_hbm, gated, scales,
    lengths, skip, x, z, b, c, b_turned, decay, table, spread, spread_request, requests, leaving, local_state, state,
    partial, gate, from_device, decay_out, decay_in, decays, state_out, state_in, step_out, step_in,
    slice_out, slice_in, before_out, before_in, enter_out, enter_in, square_out, square_in,
    load_sem, send_sem, recv_sem, ready,
):
    head_pos = lax.axis_index("head")
    ctx_pos = lax.axis_index("ctx")
    tokens, lanes = x.shape
    chunks = tokens // CHUNK
    width = lanes // ROWS
    state_size = b.shape[1]
    share_rows, share = slice_in.shape[1:]
    group = head_pos * ROWS // group_heads
    columns = pl.ds(pl.multiple_of(group * state_size, state_size), state_size)
    loads = [
        pltpu.make_async_copy(decay_hbm, decay, load_sem.at[0]),
        pltpu.make_async_copy(b_hbm.at[:, columns], b, load_sem.at[1]),
        pltpu.make_async_copy(x_hbm, x, load_sem.at[2]),
        pltpu.make_async_copy(c_hbm.at[:, columns], c, load_sem.at[3]),
        pltpu.make_async_copy(z_hbm, z, load_sem.at[4]),
        pltpu.make_async_copy(skip_hbm, skip, load_sem.at[5]),
        pltpu.make_async_copy(lengths_hbm, lengths, load_sem.at[6]),
    ]
    for i in (6, 0, 1, 2, 3, 4, 5):
        loads[i].start()

    barrier = pltpu.get_barrier_semaphore()

    side = math.isqrt(nc // 2)
    core = lax.rem(ctx_pos, 2)
    chip = ctx_pos // 2
    chip_row, chip_column = chip // side, lax.rem(chip, side)
    not_first_row, not_last_row = chip_row > 0, chip_row < side - 1

    def device_at(down, along):
        return (lax.rem(chip_row + down, side) * side + lax.rem(chip_column + along, side)) * 2 + core

    def signal_ctx(other):
        pl.semaphore_signal(barrier, inc=1, device_id={"ctx": other}, device_id_type=MESH)

    def signal_heads(semaphore, distance):
        for offset in (distance, nh - distance):
            pl.semaphore_signal(
                semaphore, inc=1, device_id={"head": lax.rem(head_pos + offset, nh)}, device_id_type=MESH
            )

    signal_ctx(ctx_pos + 1 - 2 * core)
    for along in range(1, side):
        signal_ctx(device_at(0, along))
        signal_ctx(device_at(0, along) + 1 - 2 * core)
    signal_ctx(device_at(side - 1, 0))
    signal_heads(barrier, 1)
    rounds = [2**i for i in range(nh.bit_length()) if 2 * 2**i < nh]

    waits = []

    def send(device, source, target, which, condition=None):
        copy = pltpu.make_async_remote_copy(
            src_ref=source,
            dst_ref=target,
            send_sem=send_sem.at[len(waits)],
            recv_sem=recv_sem.at[which],
            device_id=device,
            device_id_type=MESH,
        )
        waits.append((copy, condition))
        if condition is None:
            copy.start()
        else:
            pl.when(condition)(copy.start)

    def await_bytes(buffer, which):
        pltpu.make_async_remote_copy(
            src_ref=buffer,
            dst_ref=buffer,
            send_sem=send_sem.at[0],
            recv_sem=recv_sem.at[which],
            device_id={"ctx": ctx_pos + 1 - 2 * core},
            device_id_type=MESH,
        ).wait_recv()

    twin = {"ctx": ctx_pos + 1 - 2 * core}

    loads[6].wait()
    starts = []
    running = jnp.int32(0)
    for r in range(lengths.shape[0]):
        starts.append(running)
        running = running + lengths[r]

    def request_at(position):
        total = jnp.zeros(position.shape, F32)
        for start in starts:
            total = total + jnp.where(position >= start, 1.0, 0.0)
        return total

    chunk_first = ctx_pos * tokens + iota((chunks, CHUNK), 0) * CHUNK
    request = request_at(chunk_first + iota((chunks, CHUNK), 1))
    request_end = request_at(chunk_first + (CHUNK - 1))
    request_prior = request_at(chunk_first - 1)
    live_end = jnp.where(request == request_end, 1.0, 0.0)
    live_start = jnp.where(request == request_prior, 1.0, 0.0)
    requests[...] = request

    row = iota((CHUNK, lanes), 0)
    row = jnp.where(row >= HALF, row - HALF, row)
    head_of_lane = iota((CHUNK, lanes), 1) // width
    for kind in range(KINDS):
        spread[kind] = jnp.where(row == kind * ROWS + head_of_lane, 1.0, 0.0).astype(BF16)
    spread_request[...] = jnp.where(iota((CHUNK, CHUNK), 0) == REQUEST_ROW, 1.0, 0.0).astype(BF16)

    loads[0].wait()
    upper = jnp.where(iota((CHUNK, CHUNK), 0) <= iota((CHUNK, CHUNK), 1), 1.0, 0.0)
    stacked = jnp.concatenate([decay[:, k * CHUNK : (k + 1) * CHUNK] for k in range(chunks)], axis=0)
    cum = jnp.dot(stacked, upper, preferred_element_type=F32, precision=lax.Precision.HIGHEST)
    before = jnp.ones((ROWS, CHUNK), F32)
    for k in range(chunks):
        part = cum[k * ROWS : (k + 1) * ROWS]
        middle = jnp.broadcast_to(part[:, HALF - 1 : HALF], part.shape)
        end = jnp.broadcast_to(part[:, CHUNK - 1 :], part.shape)
        from_start = jnp.exp(part) * live_start[k : k + 1]
        factors = [
            jnp.exp(end - part) * live_end[k : k + 1],
            jnp.exp(middle - part),
            jnp.exp(part - middle),
            from_start,
            from_start * before,
        ]
        before = before * jnp.broadcast_to(from_start[:, CHUNK - 1 :], part.shape)
        values = jnp.concatenate(factors, axis=0)
        high = values.astype(BF16).astype(F32)
        request_rows = jnp.broadcast_to(request[k : k + 1], (ROWS, CHUNK))
        blank = jnp.zeros((HALF - REQUEST_ROW - ROWS, CHUNK), F32)
        blank_low = jnp.zeros((HALF - REQUEST_ROW, CHUNK), F32)
        whole = jnp.concatenate([high, request_rows, blank, values - high, blank_low], axis=0)
        table[k] = whole.T.astype(BF16)
    decay_out[...] = table[chunks - 1, CHUNK - 16 :, :].astype(F32)[15:16]
    leaving[...] = matmul(table[:, CHUNK - 16 :, :].reshape(16 * chunks, CHUNK), spread[FROM_CHUNK])

    loads[1].wait()
    for k in range(chunks):
        b_turned[k] = b[k * CHUNK : (k + 1) * CHUNK, :].T
    loads[2].wait()
    mine = pl.ds(pl.multiple_of(core * share, share), share)
    others = pl.ds(pl.multiple_of((1 - core) * share, share), share)
    for half, part, which in ((1 - core, others, FIRST_HALF), (core, mine, SECOND_HALF)):
        entering = jnp.zeros((state_size, share), F32)
        for k in range(chunks):
            rows = slice(k * CHUNK, (k + 1) * CHUNK)
            local_state[k, :, part] = entering.astype(BF16)
            scaled = (x[rows, part].astype(F32) * matmul(table[k], spread[TO_END, :, part])).astype(BF16)
            entering = leaving[16 * k + 15 : 16 * k + 16, part] * entering + matmul(b_turned[k], scaled)
        state_out[half] = entering
        if which == FIRST_HALF:
            pl.semaphore_wait(barrier, 2 * side + 2)
            if rounds:
                signal_heads(ready.at[0], rounds[0])
            send(twin, decay_out, decay_in, DECAY)
        send(twin, state_out.at[half], state_in.at[half], which, None if which == FIRST_HALF else core == 0)

    await_bytes(decay_in, DECAY)
    both = jnp.concatenate([decay_out[...], decay_in[...]] * (ROWS // 2), axis=0).astype(BF16)
    decays[...] = matmul(both, spread[FROM_DEVICE])
    await_bytes(state_in.at[0], FIRST_HALF)
    first_core = core == 0
    own_state, own_decay = state_out[core], decays[0:1, mine]
    got_state, got_decay = state_in[core], decays[1:2, mine]
    joined = jnp.where(first_core, own_state, got_state) * jnp.where(first_core, got_decay, own_decay)
    joined = joined + jnp.where(first_core, got_state, own_state)
    step_out[...] = own_decay * got_decay
    for i in range(side):
        slice_out[i] = joined[i * share_rows : (i + 1) * share_rows]
    for along in sorted(range(1, side), key=lambda along: -around(along, side)):
        other = device_at(0, along)
        column = lax.rem(chip_column + along, side)
        send({"ctx": other}, step_out, step_in.at[chip_column], STEP)
        send({"ctx": other}, slice_out.at[column], slice_in.at[chip_column], SLICE)
    step_in[chip_column] = step_out[...]
    slice_in[chip_column] = slice_out[chip_column]

    loads[3].wait()
    loads[4].wait()
    loads[5].wait()
    lane_head = iota((1, lanes), 1) // width
    skip_row = jnp.zeros((1, lanes), F32)
    for h in range(ROWS):
        skip_row = jnp.where(lane_head == h, skip[h], skip_row)
    causal = iota((CHUNK, CHUNK), 0) >= iota((CHUNK, CHUNK), 1)

    def own_part(k):
        rows = slice(k * CHUNK, (k + 1) * CHUNK)
        maps = c[rows, :]
        same = matmul(table[k], spread_request[...]) == requests[k : k + 1, :]
        scores = jnp.where(causal & same, matmul(maps, b_turned[k]), 0.0).astype(BF16)
        wide = x[rows, :].astype(F32)
        keys = (wide * matmul(table[k], spread[TO_KEY])).astype(BF16)
        total = matmul(scores, keys) * matmul(table[k], spread[TO_QUERY])
        total += matmul(maps, local_state[k]) * matmul(table[k], spread[FROM_CHUNK])
        partial[rows, :] = total + skip_row * wide
        from_device[rows, :] = matmul(table[k], spread[FROM_DEVICE])
        branch = z[rows, :].astype(F32)
        gate[rows, :] = branch / (1.0 + jnp.exp(-branch))

    for k in range(chunks):
        own_part(k)

    def hear(i):
        pl.semaphore_wait(ready.at[i], 2)
        if i + 1 < len(rounds):
            signal_heads(ready.at[i + 1], rounds[i + 1])

    for i in range(len(rounds))[:1]:
        hear(i)

    await_bytes(step_in.at[0 : side - 1], STEP)
    await_bytes(slice_in.at[0 : side - 1], SLICE)
    leaving_row = slice_in[0]
    for i in range(1, side):
        leaving_row = step_in[i] * leaving_row + slice_in[i]
    before_out[...] = leaving_row
    send({"ctx": device_at(1, 0)}, before_out, before_in, BEFORE, not_last_row)

    @pl.when(not_first_row)
    def _():
        await_bytes(before_in, BEFORE)

    @pl.when(chip_row == 0)
    def _():
        before_in[...] = jnp.zeros(before_in.shape, F32)

    entering = before_in[...]
    for i in range(side):
        enter_out[i] = entering
        if i < side - 1:
            entering = step_in[i] * entering + slice_in[i]
    for along in sorted(range(side), key=lambda along: -around(along, side)):
        column = lax.rem(chip_column + along, side)
        for turn in (0, 1) if along else (1,):
            send(
                {"ctx": device_at(0, along) + turn * (1 - 2 * core)}, enter_out.at[column],
                enter_in.at[core * side + chip_column], ENTER, not_first_row | (column > 0),
            )
    for i in range(len(rounds))[1:2]:
        hear(i)

    @pl.when(chip > 0)
    def _():
        enter_in[core * side + chip_column] = enter_out[chip_column]
        await_bytes(enter_in.at[0 : 2 * side - 1], ENTER)
        for half in range(2):
            part = enter_in[half * side : (half + 1) * side]
            state[:, half * share : (half + 1) * share] = part.reshape(state_size, share)

    @pl.when(chip == 0)
    def _():
        state[...] = jnp.zeros(state.shape, F32)

    @pl.when(core == 1)
    def _():
        await_bytes(state_in.at[0], SECOND_HALF)
        before_core = jnp.concatenate([state_in[0], state_in[1]], axis=1)
        state[...] = decays[1:2, :] * state[...] + before_core

    entered = state[...].astype(BF16)

    step_rows = 2 * CHUNK
    for k in range(tokens // step_rows):
        rows = slice(k * step_rows, (k + 1) * step_rows)
        output = partial[rows, :] + matmul(c[rows, :], entered) * from_device[rows, :]
        gates = output.astype(BF16).astype(F32) * gate[rows, :]
        gated[rows, :] = gates
        squared = gates * gates
        folded = squared[:, :CHUNK]
        for i in range(1, lanes // CHUNK):
            folded = folded + squared[:, i * CHUNK : (i + 1) * CHUNK]
        for i in range(2):
            square_out[2 * k + i : 2 * k + i + 1, :] = jnp.sum(
                folded[i * CHUNK : (i + 1) * CHUNK].T, axis=0, keepdims=True
            )

    for i in range(len(rounds))[2:]:
        hear(i)
    for offset in sorted(range(1, nh), key=lambda offset: -around(offset, nh)):
        send({"head": lax.rem(head_pos + offset, nh)}, square_out, square_in.at[head_pos], SQUARE)
    square_in[head_pos] = square_out[...]
    await_bytes(square_in.at[0 : nh - 1], SQUARE)
    squares = square_in[0]
    for i in range(1, nh):
        squares = squares + square_in[i]
    scales[...] = lax.rsqrt(squares / (nh * lanes) + EPS)
    for copy, condition in waits:
        if condition is None:
            copy.wait_send()
        else:
            pl.when(condition)(copy.wait_send)


def normalize(gated, scales, gain, out_hbm, out, sem):
    tokens, lanes = gated.shape
    copies = []
    for k in range(tokens // CHUNK):
        rows = slice(k * CHUNK, (k + 1) * CHUNK)
        scale = jnp.broadcast_to(scales[k : k + 1, :], (CHUNK, CHUNK)).T
        scale = jnp.concatenate([scale] * (lanes // CHUNK), axis=1)
        out[rows, :] = (gated[rows, :] * scale * gain[...]).astype(BF16)
        copies.append(pltpu.make_async_copy(out.at[rows, :], out_hbm.at[rows, :], sem.at[k]))
        copies[-1].start()
    for copy in copies:
        copy.wait()


def on_device(nh, nc, head_inputs, gate_z, input_b, output_c, log_decay, lengths, skip_coef, norm_gain):
    tokens, lanes = head_inputs.shape
    heads = skip_coef.shape[0]
    assert heads == ROWS and tokens == ROWS * CHUNK
    state_size = CHUNK
    groups = input_b.shape[1] // state_size
    chunks = tokens // CHUNK
    share = lanes // 2
    side = math.isqrt(nc // 2)
    share_rows = state_size // side
    vmem, smem, hbm = pltpu.VMEM, pltpu.SMEM, pltpu.HBM
    gated, scales = pl.pallas_call(
        functools.partial(kernel, nh, nc, heads * nh // groups),
        out_shape=(
            jax.ShapeDtypeStruct((tokens, lanes), F32),
            jax.ShapeDtypeStruct((chunks, CHUNK), F32),
        ),
        in_specs=[pl.BlockSpec(memory_space=hbm)] * 7,
        out_specs=(pl.BlockSpec(memory_space=vmem), pl.BlockSpec(memory_space=vmem)),
        scratch_shapes=[
            smem(lengths.shape, jnp.int32),
            smem(skip_coef.shape, F32),
            vmem((tokens, lanes), BF16),
            vmem((tokens, lanes), BF16),
            vmem((tokens, state_size), BF16),
            vmem((tokens, state_size), BF16),
            vmem((chunks, state_size, CHUNK), BF16),
            vmem((heads, tokens), F32),
            vmem((chunks, CHUNK, CHUNK), BF16),
            vmem((KINDS, CHUNK, lanes), BF16),
            vmem((CHUNK, CHUNK), BF16),
            vmem((chunks, CHUNK), F32),
            vmem((16 * chunks, lanes), F32),
            vmem((chunks, state_size, lanes), BF16),
            vmem((state_size, lanes), F32),
            vmem((tokens, lanes), F32),
            vmem((tokens, lanes), F32),
            vmem((tokens, lanes), F32),
            vmem((1, CHUNK), F32),
            vmem((1, CHUNK), F32),
            vmem((heads, lanes), F32),
            vmem((2, state_size, share), F32),
            vmem((2, state_size, share), F32),
            vmem((1, share), F32),
            vmem((side, 1, share), F32),
            vmem((side, share_rows, share), F32),
            vmem((side, share_rows, share), F32),
            vmem((share_rows, share), F32),
            vmem((share_rows, share), F32),
            vmem((side, share_rows, share), F32),
            vmem((2 * side, share_rows, share), F32),
            vmem((chunks, CHUNK), F32),
            vmem((nh, chunks, CHUNK), F32),
            pltpu.SemaphoreType.DMA((7,)),
            pltpu.SemaphoreType.DMA((6 * side + nh + 4,)),
            pltpu.SemaphoreType.DMA((10,)),
            pltpu.SemaphoreType.REGULAR((4,)),
        ],
        compiler_params=pltpu.CompilerParams(
            collective_id=0, has_side_effects=True, vmem_limit_bytes=24 << 20
        ),
    )(*(
        pltpu.with_memory_space_constraint(operand, hbm)
        for operand in (lengths, skip_coef, head_inputs, gate_z, input_b, output_c, log_decay.T)
    ))
    return pl.pallas_call(
        normalize,
        out_shape=jax.ShapeDtypeStruct((tokens, lanes), BF16),
        in_specs=[pl.BlockSpec(memory_space=vmem)] * 3,
        out_specs=pl.BlockSpec(memory_space=hbm),
        scratch_shapes=[vmem((tokens, lanes), BF16), pltpu.SemaphoreType.DMA((chunks,))],
        compiler_params=pltpu.CompilerParams(vmem_limit_bytes=8 << 20),
    )(gated, scales, norm_gain.reshape(1, lanes))


def solution(mesh):
    return jax.shard_map(
        functools.partial(on_device, mesh.shape["head"], mesh.shape["ctx"]),
        mesh=mesh,
        in_specs=(
            P("ctx", "head"),
            P("ctx", "head"),
            P("ctx", None),
            P("ctx", None),
            P("ctx", "head"),
            P(),
            P("head"),
            P("head"),
        ),
        out_specs=P("ctx", "head"),
        check_vma=False,
    )
```

```python
import functools
import math

import jax
import jax.numpy as jnp
from jax import lax
from jax.experimental import pallas as pl
from jax.experimental.pallas import tpu as pltpu
from jax.sharding import PartitionSpec as P

MESH = pl.DeviceIdType.MESH
CHUNK = 128
HALF = CHUNK // 2
ROWS = 8
EPS = 1e-05
TO_END, TO_KEY, TO_QUERY, FROM_CHUNK, FROM_DEVICE = range(5)
KINDS = 5
REQUEST_ROW = KINDS * ROWS
DECAY, FIRST_HALF, SECOND_HALF, BEFORE, STEP, SLICE, ENTER, SQUARE = range(8)
F32, BF16 = jnp.float32, jnp.bfloat16


def iota(shape, dim):
    return lax.broadcasted_iota(jnp.int32, shape, dim)


def matmul(left, right):
    return jnp.dot(left, right, preferred_element_type=F32)


def around(offset, count):
    return min(offset, count - offset)


def kernel(
    nh, nc, group_heads, lengths_hbm, skip_hbm, x_hbm, z_hbm, b_hbm, c_hbm, decay_hbm, gated, scales,
    lengths, skip, x, z, b, c, b_turned, decay, table, spread, spread_request, requests, leaving, local_state, state,
    partial, gate, from_device, decay_out, decay_in, decays, state_out, state_in, step_out, step_in,
    slice_out, slice_in, before_out, before_in, enter_out, enter_in, square_out, square_in,
    load_sem, send_sem, recv_sem, ready,
):
    head_pos = lax.axis_index("head")
    ctx_pos = lax.axis_index("ctx")
    tokens, lanes = x.shape
    chunks = tokens // CHUNK
    width = lanes // ROWS
    state_size = b.shape[1]
    share_rows, share = slice_in.shape[1:]
    group = head_pos * ROWS // group_heads
    columns = pl.ds(pl.multiple_of(group * state_size, state_size), state_size)
    loads = [
        pltpu.make_async_copy(decay_hbm, decay, load_sem.at[0]),
        pltpu.make_async_copy(b_hbm.at[:, columns], b, load_sem.at[1]),
        pltpu.make_async_copy(x_hbm, x, load_sem.at[2]),
        pltpu.make_async_copy(c_hbm.at[:, columns], c, load_sem.at[3]),
        pltpu.make_async_copy(z_hbm, z, load_sem.at[4]),
        pltpu.make_async_copy(skip_hbm, skip, load_sem.at[5]),
        pltpu.make_async_copy(lengths_hbm, lengths, load_sem.at[6]),
    ]
    for i in (6, 0, 1, 2):
        loads[i].start()

    barrier = pltpu.get_barrier_semaphore()

    side = math.isqrt(nc // 2)
    core = lax.rem(ctx_pos, 2)
    chip = ctx_pos // 2
    chip_row, chip_column = chip // side, lax.rem(chip, side)
    not_first_row, not_last_row = chip_row > 0, chip_row < side - 1

    def device_at(down, along):
        return (lax.rem(chip_row + down, side) * side + lax.rem(chip_column + along, side)) * 2 + core

    def signal_ctx(other):
        pl.semaphore_signal(barrier, inc=1, device_id={"ctx": other}, device_id_type=MESH)

    def signal_heads(semaphore, distance):
        for offset in (distance, nh - distance):
            pl.semaphore_signal(
                semaphore, inc=1, device_id={"head": lax.rem(head_pos + offset, nh)}, device_id_type=MESH
            )

    signal_ctx(ctx_pos + 1 - 2 * core)
    for along in range(1, side):
        signal_ctx(device_at(0, along))
        signal_ctx(device_at(0, along) + 1 - 2 * core)
    signal_ctx(device_at(side - 1, 0))
    signal_heads(barrier, 1)
    rounds = [2**i for i in range(nh.bit_length()) if 2 * 2**i < nh]

    waits = []

    def send(device, source, target, which, condition=None):
        copy = pltpu.make_async_remote_copy(
            src_ref=source,
            dst_ref=target,
            send_sem=send_sem.at[len(waits)],
            recv_sem=recv_sem.at[which],
            device_id=device,
            device_id_type=MESH,
        )
        waits.append((copy, condition))
        if condition is None:
            copy.start()
        else:
            pl.when(condition)(copy.start)

    def await_bytes(buffer, which):
        pltpu.make_async_remote_copy(
            src_ref=buffer,
            dst_ref=buffer,
            send_sem=send_sem.at[0],
            recv_sem=recv_sem.at[which],
            device_id={"ctx": ctx_pos + 1 - 2 * core},
            device_id_type=MESH,
        ).wait_recv()

    twin = {"ctx": ctx_pos + 1 - 2 * core}

    loads[6].wait()
    starts = []
    running = jnp.int32(0)
    for r in range(lengths.shape[0]):
        starts.append(running)
        running = running + lengths[r]

    def request_at(position):
        total = jnp.zeros(position.shape, F32)
        for start in starts:
            total = total + jnp.where(position >= start, 1.0, 0.0)
        return total

    chunk_first = ctx_pos * tokens + iota((chunks, CHUNK), 0) * CHUNK
    request = request_at(chunk_first + iota((chunks, CHUNK), 1))
    request_end = request_at(chunk_first + (CHUNK - 1))
    request_prior = request_at(chunk_first - 1)
    live_end = jnp.where(request == request_end, 1.0, 0.0)
    live_start = jnp.where(request == request_prior, 1.0, 0.0)
    requests[...] = request

    row = iota((CHUNK, lanes), 0)
    row = jnp.where(row >= HALF, row - HALF, row)
    head_of_lane = iota((CHUNK, lanes), 1) // width
    for kind in range(KINDS):
        spread[kind] = jnp.where(row == kind * ROWS + head_of_lane, 1.0, 0.0).astype(BF16)
    spread_request[...] = jnp.where(iota((CHUNK, CHUNK), 0) == REQUEST_ROW, 1.0, 0.0).astype(BF16)

    loads[0].wait()
    upper = jnp.where(iota((CHUNK, CHUNK), 0) <= iota((CHUNK, CHUNK), 1), 1.0, 0.0)
    stacked = jnp.concatenate([decay[:, k * CHUNK : (k + 1) * CHUNK] for k in range(chunks)], axis=0)
    cum = jnp.dot(stacked, upper, preferred_element_type=F32, precision=lax.Precision.HIGHEST)
    before = jnp.ones((ROWS, CHUNK), F32)
    for k in range(chunks):
        part = cum[k * ROWS : (k + 1) * ROWS]
        middle = jnp.broadcast_to(part[:, HALF - 1 : HALF], part.shape)
        end = jnp.broadcast_to(part[:, CHUNK - 1 :], part.shape)
        from_start = jnp.exp(part) * live_start[k : k + 1]
        factors = [
            jnp.exp(end - part) * live_end[k : k + 1],
            jnp.exp(middle - part),
            jnp.exp(part - middle),
            from_start,
            from_start * before,
        ]
        before = before * jnp.broadcast_to(from_start[:, CHUNK - 1 :], part.shape)
        values = jnp.concatenate(factors, axis=0)
        high = values.astype(BF16).astype(F32)
        request_rows = jnp.broadcast_to(request[k : k + 1], (ROWS, CHUNK))
        blank = jnp.zeros((HALF - REQUEST_ROW - ROWS, CHUNK), F32)
        blank_low = jnp.zeros((HALF - REQUEST_ROW, CHUNK), F32)
        whole = jnp.concatenate([high, request_rows, blank, values - high, blank_low], axis=0)
        table[k] = whole.T.astype(BF16)
    decay_out[...] = table[chunks - 1, CHUNK - 16 :, :].astype(F32)[15:16]
    leaving[...] = matmul(table[:, CHUNK - 16 :, :].reshape(16 * chunks, CHUNK), spread[FROM_CHUNK])

    loads[1].wait()
    for k in range(chunks):
        b_turned[k] = b[k * CHUNK : (k + 1) * CHUNK, :].T
    loads[2].wait()
    for i in (3, 4, 5):
        loads[i].start()
    mine = pl.ds(pl.multiple_of(core * share, share), share)
    others = pl.ds(pl.multiple_of((1 - core) * share, share), share)
    for half, part, which in ((1 - core, others, FIRST_HALF), (core, mine, SECOND_HALF)):
        entering = jnp.zeros((state_size, share), F32)
        for k in range(chunks):
            rows = slice(k * CHUNK, (k + 1) * CHUNK)
            local_state[k, :, part] = entering.astype(BF16)
            scaled = (x[rows, part].astype(F32) * matmul(table[k], spread[TO_END, :, part])).astype(BF16)
            entering = leaving[16 * k + 15 : 16 * k + 16, part] * entering + matmul(b_turned[k], scaled)
        state_out[half] = entering
        if which == FIRST_HALF:
            pl.semaphore_wait(barrier, 2 * side + 2)
            if rounds:
                signal_heads(ready.at[0], rounds[0])
            send(twin, decay_out, decay_in, DECAY)
        send(twin, state_out.at[half], state_in.at[half], which, None if which == FIRST_HALF else core == 0)

    await_bytes(decay_in, DECAY)
    both = jnp.concatenate([decay_out[...], decay_in[...]] * (ROWS // 2), axis=0).astype(BF16)
    decays[...] = matmul(both, spread[FROM_DEVICE])
    await_bytes(state_in.at[0], FIRST_HALF)
    first_core = core == 0
    own_state, own_decay = state_out[core], decays[0:1, mine]
    got_state, got_decay = state_in[core], decays[1:2, mine]
    joined = jnp.where(first_core, own_state, got_state) * jnp.where(first_core, got_decay, own_decay)
    joined = joined + jnp.where(first_core, got_state, own_state)
    step_out[...] = own_decay * got_decay
    for i in range(side):
        slice_out[i] = joined[i * share_rows : (i + 1) * share_rows]
    for along in sorted(range(1, side), key=lambda along: -around(along, side)):
        other = device_at(0, along)
        column = lax.rem(chip_column + along, side)
        send({"ctx": other}, step_out, step_in.at[chip_column], STEP)
        send({"ctx": other}, slice_out.at[column], slice_in.at[chip_column], SLICE)
    step_in[chip_column] = step_out[...]
    slice_in[chip_column] = slice_out[chip_column]

    loads[3].wait()
    loads[4].wait()
    loads[5].wait()
    lane_head = iota((1, lanes), 1) // width
    skip_row = jnp.zeros((1, lanes), F32)
    for h in range(ROWS):
        skip_row = jnp.where(lane_head == h, skip[h], skip_row)
    causal = iota((CHUNK, CHUNK), 0) >= iota((CHUNK, CHUNK), 1)

    def own_part(k):
        rows = slice(k * CHUNK, (k + 1) * CHUNK)
        maps = c[rows, :]
        same = matmul(table[k], spread_request[...]) == requests[k : k + 1, :]
        scores = jnp.where(causal & same, matmul(maps, b_turned[k]), 0.0).astype(BF16)
        wide = x[rows, :].astype(F32)
        keys = (wide * matmul(table[k], spread[TO_KEY])).astype(BF16)
        total = matmul(scores, keys) * matmul(table[k], spread[TO_QUERY])
        total += matmul(maps, local_state[k]) * matmul(table[k], spread[FROM_CHUNK])
        partial[rows, :] = total + skip_row * wide
        from_device[rows, :] = matmul(table[k], spread[FROM_DEVICE])
        branch = z[rows, :].astype(F32)
        gate[rows, :] = branch / (1.0 + jnp.exp(-branch))

    for k in range(chunks):
        own_part(k)

    def hear(i):
        pl.semaphore_wait(ready.at[i], 2)
        if i + 1 < len(rounds):
            signal_heads(ready.at[i + 1], rounds[i + 1])

    for i in range(len(rounds))[:1]:
        hear(i)

    await_bytes(step_in.at[0 : side - 1], STEP)
    await_bytes(slice_in.at[0 : side - 1], SLICE)
    leaving_row = slice_in[0]
    for i in range(1, side):
        leaving_row = step_in[i] * leaving_row + slice_in[i]
    before_out[...] = leaving_row
    send({"ctx": device_at(1, 0)}, before_out, before_in, BEFORE, not_last_row)

    @pl.when(not_first_row)
    def _():
        await_bytes(before_in, BEFORE)

    @pl.when(chip_row == 0)
    def _():
        before_in[...] = jnp.zeros(before_in.shape, F32)

    entering = before_in[...]
    for i in range(side):
        enter_out[i] = entering
        if i < side - 1:
            entering = step_in[i] * entering + slice_in[i]
    for along in sorted(range(side), key=lambda along: -around(along, side)):
        column = lax.rem(chip_column + along, side)
        for turn in (0, 1) if along else (1,):
            send(
                {"ctx": device_at(0, along) + turn * (1 - 2 * core)}, enter_out.at[column],
                enter_in.at[core * side + chip_column], ENTER, not_first_row | (column > 0),
            )
    for i in range(len(rounds))[1:2]:
        hear(i)

    @pl.when(chip > 0)
    def _():
        enter_in[core * side + chip_column] = enter_out[chip_column]
        await_bytes(enter_in.at[0 : 2 * side - 1], ENTER)
        for half in range(2):
            part = enter_in[half * side : (half + 1) * side]
            state[:, half * share : (half + 1) * share] = part.reshape(state_size, share)

    @pl.when(chip == 0)
    def _():
        state[...] = jnp.zeros(state.shape, F32)

    @pl.when(core == 1)
    def _():
        await_bytes(state_in.at[0], SECOND_HALF)
        before_core = jnp.concatenate([state_in[0], state_in[1]], axis=1)
        state[...] = decays[1:2, :] * state[...] + before_core

    entered = state[...].astype(BF16)

    step_rows = 2 * CHUNK
    for k in range(tokens // step_rows):
        rows = slice(k * step_rows, (k + 1) * step_rows)
        output = partial[rows, :] + matmul(c[rows, :], entered) * from_device[rows, :]
        gates = output.astype(BF16).astype(F32) * gate[rows, :]
        gated[rows, :] = gates
        squared = gates * gates
        folded = squared[:, :CHUNK]
        for i in range(1, lanes // CHUNK):
            folded = folded + squared[:, i * CHUNK : (i + 1) * CHUNK]
        for i in range(2):
            square_out[2 * k + i : 2 * k + i + 1, :] = jnp.sum(
                folded[i * CHUNK : (i + 1) * CHUNK].T, axis=0, keepdims=True
            )

    for i in range(len(rounds))[2:]:
        hear(i)
    for offset in sorted(range(1, nh), key=lambda offset: -around(offset, nh)):
        send({"head": lax.rem(head_pos + offset, nh)}, square_out, square_in.at[head_pos], SQUARE)
    square_in[head_pos] = square_out[...]
    await_bytes(square_in.at[0 : nh - 1], SQUARE)
    squares = square_in[0]
    for i in range(1, nh):
        squares = squares + square_in[i]
    scales[...] = lax.rsqrt(squares / (nh * lanes) + EPS)
    for copy, condition in waits:
        if condition is None:
            copy.wait_send()
        else:
            pl.when(condition)(copy.wait_send)


def normalize(gated, scales, gain, out_hbm, out, sem):
    tokens, lanes = gated.shape
    copies = []
    for k in range(tokens // CHUNK):
        rows = slice(k * CHUNK, (k + 1) * CHUNK)
        scale = jnp.broadcast_to(scales[k : k + 1, :], (CHUNK, CHUNK)).T
        scale = jnp.concatenate([scale] * (lanes // CHUNK), axis=1)
        out[rows, :] = (gated[rows, :] * scale * gain[...]).astype(BF16)
        copies.append(pltpu.make_async_copy(out.at[rows, :], out_hbm.at[rows, :], sem.at[k]))
        copies[-1].start()
    for copy in copies:
        copy.wait()


def on_device(nh, nc, head_inputs, gate_z, input_b, output_c, log_decay, lengths, skip_coef, norm_gain):
    tokens, lanes = head_inputs.shape
    heads = skip_coef.shape[0]
    assert heads == ROWS and tokens == ROWS * CHUNK
    state_size = CHUNK
    groups = input_b.shape[1] // state_size
    chunks = tokens // CHUNK
    share = lanes // 2
    side = math.isqrt(nc // 2)
    share_rows = state_size // side
    vmem, smem, hbm = pltpu.VMEM, pltpu.SMEM, pltpu.HBM
    gated, scales = pl.pallas_call(
        functools.partial(kernel, nh, nc, heads * nh // groups),
        out_shape=(
            jax.ShapeDtypeStruct((tokens, lanes), F32),
            jax.ShapeDtypeStruct((chunks, CHUNK), F32),
        ),
        in_specs=[pl.BlockSpec(memory_space=hbm)] * 7,
        out_specs=(pl.BlockSpec(memory_space=vmem), pl.BlockSpec(memory_space=vmem)),
        scratch_shapes=[
            smem(lengths.shape, jnp.int32),
            smem(skip_coef.shape, F32),
            vmem((tokens, lanes), BF16),
            vmem((tokens, lanes), BF16),
            vmem((tokens, state_size), BF16),
            vmem((tokens, state_size), BF16),
            vmem((chunks, state_size, CHUNK), BF16),
            vmem((heads, tokens), F32),
            vmem((chunks, CHUNK, CHUNK), BF16),
            vmem((KINDS, CHUNK, lanes), BF16),
            vmem((CHUNK, CHUNK), BF16),
            vmem((chunks, CHUNK), F32),
            vmem((16 * chunks, lanes), F32),
            vmem((chunks, state_size, lanes), BF16),
            vmem((state_size, lanes), F32),
            vmem((tokens, lanes), F32),
            vmem((tokens, lanes), F32),
            vmem((tokens, lanes), F32),
            vmem((1, CHUNK), F32),
            vmem((1, CHUNK), F32),
            vmem((heads, lanes), F32),
            vmem((2, state_size, share), F32),
            vmem((2, state_size, share), F32),
            vmem((1, share), F32),
            vmem((side, 1, share), F32),
            vmem((side, share_rows, share), F32),
            vmem((side, share_rows, share), F32),
            vmem((share_rows, share), F32),
            vmem((share_rows, share), F32),
            vmem((side, share_rows, share), F32),
            vmem((2 * side, share_rows, share), F32),
            vmem((chunks, CHUNK), F32),
            vmem((nh, chunks, CHUNK), F32),
            pltpu.SemaphoreType.DMA((7,)),
            pltpu.SemaphoreType.DMA((6 * side + nh + 4,)),
            pltpu.SemaphoreType.DMA((10,)),
            pltpu.SemaphoreType.REGULAR((4,)),
        ],
        compiler_params=pltpu.CompilerParams(
            collective_id=0, has_side_effects=True, vmem_limit_bytes=24 << 20
        ),
    )(*(
        pltpu.with_memory_space_constraint(operand, hbm)
        for operand in (lengths, skip_coef, head_inputs, gate_z, input_b, output_c, log_decay.T)
    ))
    return pl.pallas_call(
        normalize,
        out_shape=jax.ShapeDtypeStruct((tokens, lanes), BF16),
        in_specs=[pl.BlockSpec(memory_space=vmem)] * 3,
        out_specs=pl.BlockSpec(memory_space=hbm),
        scratch_shapes=[vmem((tokens, lanes), BF16), pltpu.SemaphoreType.DMA((chunks,))],
        compiler_params=pltpu.CompilerParams(vmem_limit_bytes=8 << 20),
    )(gated, scales, norm_gain.reshape(1, lanes))


def solution(mesh):
    return jax.shard_map(
        functools.partial(on_device, mesh.shape["head"], mesh.shape["ctx"]),
        mesh=mesh,
        in_specs=(
            P("ctx", "head"),
            P("ctx", "head"),
            P("ctx", None),
            P("ctx", None),
            P("ctx", "head"),
            P(),
            P("head"),
            P("head"),
        ),
        out_specs=P("ctx", "head"),
        check_vma=False,
    )
```
